256 devices in a mesh: rep: 16 (over y, z_lo), fsdp: 16 (over z_hi, x, core).
Axes of the slice: x: 4, y: 4, z: 8 (z_hi: 2, z_lo: 4; z = z_hi * 4 + z_lo), core: 2. Of those that a mesh axis runs over, the one named last changes fastest.
Arguments:
- hidden_in: bfloat16 [16, 16, 256, 4096], P('rep', 'fsdp'), may hold values from -6 to 6
- scan_in: bfloat16 [16, 16, 256, 4096], P('rep', 'fsdp'), may hold values from -6 to 6
- grad_out: bfloat16 [16, 16, 256, 4096], P('rep', 'fsdp'), may hold values from -6 to 6
- episodes: int32 [16, 16, 256], P('rep', 'fsdp'), may hold values from 0 to 2, never falling along the last dimension, each value on 1 to 128 neighbouring positions
- gossip_step: int32 [1], replicated, may hold values from 0 to 63
- state_proj: float32 [16, 4096, 256], P('rep', 'fsdp'), may hold values from -0.01953125 to 0.01953125
- step_proj: float32 [16, 32, 4096], P('rep', None, 'fsdp'), may hold values from -0.09375 to 0.09375
- decay_log: float32 [16, 32], P('rep'), may hold values from -5.5 to -3
- step_bias: float32 [16, 32], P('rep'), may hold values from -1 to 1
Outputs:
- layer_grad: bfloat16 [16, 16, 256, 4096], P('rep', 'fsdp')
- scan_grad: bfloat16 [16, 16, 256, 4096], P('rep', 'fsdp')
- new_state_proj: float32 [16, 4096, 256], P('rep', 'fsdp')
- new_step_proj: float32 [16, 32, 4096], P('rep', None, 'fsdp')
- new_decay_log: float32 [16, 32], P('rep')
- new_step_bias: float32 [16, 32], P('rep')
The draws below stay inside these ranges and needn't reach their ends.
Inputs may be any that keep to these rules, and one draw needn't show every extreme that they name: `episodes`: within each sequence the episode ids never fall; an episode has at most half of 256 tokens, and one has exactly that many.
All inputs are finite; a program needn't handle non-finite values.
Results may differ from the reference program's by a relative error of at most 0.0058.
The reference program's roundings to bfloat16 on the way count: a program that leaves them out, or rounds other values in their place, can miss the bound.
Values may be sent and summed in bfloat16 or wider, within the bound.
A program may use at most 128 MiB of HBM per device.

```python
import math
import jax
import jax.numpy as jnp
import numpy as np
from jax import lax

D = 4096
HEADS = 32
HEAD_DIM = 128
STATE = 128
LEN = 256
INNER = 4096
REPS = 16
SEQS = 16


def draw_hidden_in(key, part):
    key_base, key_order, key_column = jax.random.split(key, 3)
    shape = (REPS, SEQS, LEN, D)
    block_total = 16
    order = jax.random.permutation(key_order, block_total).astype(jnp.float32)
    spread = 0.5
    level = jnp.power(10.0, spread * (2.0 * order / (block_total - 1) - 1.0))
    column = jnp.arange(D)
    block_level = level[column // (D // block_total)]
    parity = jnp.where(column % 2 == 0, 1.35, 0.55)
    rough = jnp.exp(jax.random.uniform(key_column, (D,), jnp.float32, -0.5, 0.5))
    column_scale = block_level * parity * rough * 0.61
    base = jax.random.normal(key_base, shape, jnp.float32)
    return jnp.clip(base * column_scale, -6.0, 6.0).astype(jnp.bfloat16)


def steps_of(key, extent, cuts, least, high):
    gain = 1.0
    for dim, shards_of in cuts:
        steps = jax.random.uniform(jax.random.fold_in(jax.random.fold_in(key, 6), dim), (shards_of,), jnp.float32, least / len(cuts), high / len(cuts))
        gain = gain * jnp.repeat(jnp.exp(steps), extent[dim] // shards_of).reshape((-1,) + (1,) * (len(extent) - 1 - dim))
    return gain


def length_profile(count, total, bound, skew):
    portions = [(1 << 20) // math.isqrt(rank ** skew) + 1 for rank in range(2, count + 1)]
    spare, holding = total - bound - (count - 1), [1] * (count - 1)
    while spare > 0:
        free = [i for i in range(count - 1) if holding[i] < bound]
        pool, budget = sum([portions[i] for i in free]), spare
        for i in free:
            more = min(bound - holding[i], max(1, budget * portions[i] // pool), spare)
            holding[i] = holding[i] + more
            spare = spare - more
    return np.array([bound] + holding)


def uneven_parts(stream_key, amount, total, limit, skew):
    if amount == 2:
        one = jax.random.randint(stream_key, (), max(1, total - limit), min(limit, total - 1) + 1)
        return jnp.stack([one, total - one])
    lengths = jnp.asarray(length_profile(amount, total, limit, skew), jnp.int32)
    couples = (amount - 1) // 2
    giver, taker = lengths[1:1 + 2 * couples:2], lengths[2:2 + 2 * couples:2]
    margin = jnp.minimum(giver - 1, limit - taker)
    shifted = jax.random.randint(jax.random.fold_in(stream_key, 1), (couples,), 0, 1 << 20) % (margin + 1)
    lengths = lengths.at[1:1 + 2 * couples:2].set(giver - shifted).at[2:2 + 2 * couples:2].set(taker + shifted)
    return lengths[jax.random.permutation(jax.random.fold_in(stream_key, 2), amount)]


def centred(stream_key, extent, deviation, bound, cuts=(), kind=jnp.bfloat16):
    values = deviation * jax.random.normal(stream_key, extent, jnp.float32)
    if cuts:
        values = values * steps_of(stream_key, extent, cuts, -0.22, 0.18)
    return jnp.clip(values, -bound, bound).astype(kind)


def setup_inputs(seed: int = 0) -> dict:
    key_list = jax.random.split(jax.random.key(seed), 10)
    return {
        "hidden_in": draw_hidden_in(jax.random.fold_in(key_list[9], 71), 0),
        "scan_in": centred(key_list[1], (REPS, SEQS, LEN, INNER), 1.0, 6.0, ((0, 16), (1, 16))),
        "grad_out": centred(key_list[2], (REPS, SEQS, LEN, INNER), 1.0, 6.0, ((0, 16), (1, 16))),
        "episodes": jax.vmap(lambda own: jnp.searchsorted(jnp.cumsum(uneven_parts(own, 3, LEN, LEN // 2, 0)), jnp.arange(LEN), side="right"))(jax.random.split(key_list[3], REPS * SEQS)).reshape((REPS, SEQS, LEN)).astype(jnp.int32),
        "gossip_step": jax.random.randint(key_list[4], (1,), 0, 64).astype(jnp.int32),
        "state_proj": centred(key_list[5], (REPS, D, 2 * STATE), (D * 24) ** -0.5, 0.01953125, ((0, 16), (1, 16)), jnp.float32),
        "step_proj": centred(key_list[6], (REPS, HEADS, D), D ** -0.5, 0.09375, ((0, 16), (2, 16)), jnp.float32),
        "decay_log": jnp.clip(-5.5 + 2.5 * jax.random.uniform(key_list[7], (REPS, HEADS), jnp.float32) ** steps_of(key_list[7], (REPS, HEADS), ((0, 16),), -0.2, 0.2), -5.5, -3.0),
        "step_bias": jnp.clip(jax.random.uniform(key_list[8], (REPS, HEADS), jnp.float32, -1.0, 1.0) * steps_of(key_list[8], (REPS, HEADS), ((0, 16),), -0.4, 0.0), -1.0, 1.0),
    }


learn_rate = 0.1
eps_norm = 1e-06

def scan_whole(features, values_in, decay_arg, bias_arg, episode_ids):
    length = features.shape[0]
    input_proj = features[:, :STATE]
    output_proj = features[:, STATE:2 * STATE]
    step_size = jax.nn.softplus(features[:, 2 * STATE:] + bias_arg)
    cumulative = jnp.cumsum(-jnp.exp(decay_arg) * step_size, axis=0)
    position = jnp.arange(length)
    allowed = (position[:, None] >= position[None, :]) & (episode_ids[:, None] == episode_ids[None, :])
    allowed_head = allowed[:, :, None]
    log_gap = cumulative[:, None, :] - cumulative[None, :, :]
    decay_term = jnp.where(allowed_head, jnp.exp(jnp.where(allowed_head, log_gap, 0.0)), 0.0)
    scores = jnp.dot(output_proj, input_proj.T, precision=lax.Precision.HIGHEST)
    weighting = decay_term * scores[:, :, None] * step_size[None, :, :]
    channels = values_in.astype(jnp.float32).reshape(length, HEADS, HEAD_DIM)
    result = jnp.einsum('tsh,shp->thp', weighting, channels, precision=lax.Precision.HIGHEST)
    return result.reshape(length, HEADS * HEAD_DIM)

def one_sequence(tokens_in, values_in, cotangent, episode_ids, weights_all, decay_own, bias_own):
    features = jnp.dot(tokens_in, weights_all, preferred_element_type=jnp.float32)

    def forward(feat_arg, values_arg, decay_arg, bias_arg):
        return scan_whole(feat_arg, values_arg, decay_arg, bias_arg, episode_ids)
    outputs, pullback = jax.vjp(forward, features, values_in, decay_own, bias_own)
    feat_grad, values_grad, decay_grad, bias_grad = pullback(cotangent.astype(outputs.dtype))
    feat_grad = feat_grad.astype(jnp.bfloat16)
    tokens_grad = jnp.dot(feat_grad, weights_all.T, preferred_element_type=jnp.float32).astype(jnp.bfloat16)
    return (tokens_grad, values_grad, feat_grad, decay_grad, bias_grad)

def trust_update(param, grad):
    trust_ratio = jnp.sqrt(jnp.mean(param * param)) / jnp.sqrt(jnp.mean(grad * grad) + eps_norm)
    return param - learn_rate * trust_ratio * grad

def one_replica(replica_args):
    tokens_all, values_all, cotangents, episode_all, state_own, step_own, decay_own, bias_own = replica_args
    weights_all = jnp.concatenate([state_own.astype(jnp.bfloat16), step_own.astype(jnp.bfloat16).T], axis=1)

    def per_sequence(seq_args):
        tokens_in, values_in, cotangent, episode_ids = seq_args
        return one_sequence(tokens_in, values_in, cotangent, episode_ids, weights_all, decay_own, bias_own)
    tokens_grad, values_grad, feat_grad, decay_grad, bias_grad = lax.map(per_sequence, (tokens_all, values_all, cotangents, episode_all))
    flat_tokens = tokens_all.reshape(-1, D)
    flat_grad = feat_grad.reshape(-1, feat_grad.shape[-1])
    weight_grad = lax.dot_general(flat_tokens, flat_grad, (((0,), (0,)), ((), ())), preferred_element_type=jnp.float32)
    new_state = trust_update(state_own, weight_grad[:, :2 * STATE])
    new_step = trust_update(step_own, weight_grad[:, 2 * STATE:].T)
    head_param = jnp.concatenate([decay_own, bias_own])
    head_grad = jnp.concatenate([lax.optimization_barrier(jnp.sum(decay_grad, axis=0)), lax.optimization_barrier(jnp.sum(bias_grad, axis=0))])
    new_head = trust_update(head_param, head_grad)
    return (tokens_grad, values_grad, new_state, new_step, new_head[:HEADS], new_head[HEADS:])

def reference(hidden_in, scan_in, grad_out, episodes, gossip_step, state_proj, step_proj, decay_log, step_bias):
    layer_grad, scan_grad, new_state, new_step, new_decay, new_bias = lax.map(one_replica, (hidden_in, scan_in, grad_out, episodes, state_proj, step_proj, decay_log, step_bias))
    rounds = REPS.bit_length() - 1
    bit_index = gossip_step[0] % rounds
    distance = jnp.power(jnp.full((), 2, jnp.int32), bit_index).astype(jnp.int32)
    replica = jnp.arange(REPS, dtype=jnp.int32)
    partner = jnp.where(replica // distance % 2 == 0, replica + distance, replica - distance).astype(jnp.int32)

    def mixing(values):
        return (values + jnp.take(values, partner, axis=0)) * 0.5
    return (layer_grad, scan_grad, mixing(new_state), mixing(new_step), mixing(new_decay), mixing(new_bias))
```

```python
import functools

import jax
import jax.numpy as jnp
from jax import lax
from jax.experimental import pallas as pl
from jax.experimental.pallas import tpu as pltpu
from jax.sharding import PartitionSpec as P

MESH = pl.DeviceIdType.MESH
F32 = jnp.float32
BF16 = jnp.bfloat16
HIGH = lax.Precision.HIGHEST
LOG2E = 1.4426950408889634
TINY = 1e-37
CAP = 60.0
RATE = 0.1
EPS = 1e-6
WIDTH = 128


def nn(a, b, precision=None):
    return lax.dot_general(
        a, b, (((1,), (0,)), ((), ())), precision=precision, preferred_element_type=F32
    )


def nt(a, b, precision=None):
    return lax.dot_general(
        a, b, (((1,), (1,)), ((), ())), precision=precision, preferred_element_type=F32
    )


def split3(value):
    high = value.astype(BF16).astype(F32)
    rest = value - high
    mid = rest.astype(BF16).astype(F32)
    return high, mid, rest - mid


def layer_kernel(
    dims,
    bit_ref,
    own_ref,
    state_ref,
    step_ref,
    hid_hbm,
    val_hbm,
    cot_hbm,
    epc_ref,
    epr_ref,
    acol_ref,
    bcol_ref,
    head_ref,
    lay_hbm,
    sgr_hbm,
    nstate_ref,
    nstep_ref,
    nhead_ref,
    hid,
    val,
    cot,
    wts,
    dwo,
    acc,
    from_core,
    hop1,
    hop2,
    from_z,
    part_p,
    part_g,
    part_s,
    zsend,
    gsend,
    heads_in,
    sums_in,
    final_send,
    lay,
    sgr,
    feat,
    du3,
    rhs,
    scores,
    ds0,
    ds1,
    mrow,
    mcol,
    fgt,
    fg,
    fgl,
    local_sem,
    ssem,
    rsem,
):
    heads, reps, seqs, chunk, rows = dims
    half = rows // 2
    bits = reps.bit_length() - 1
    state2 = 2 * WIDTH
    me = lax.axis_index("fsdp")
    rep = lax.axis_index("rep")
    core = lax.rem(me, 2)
    x_at = lax.rem(lax.div(me, 2), 4)
    z_at = lax.div(me, 8)

    def index_of(z, x, c):
        return z * 8 + lax.rem(x, 4) * 2 + c

    other_z = 1 - z_at
    other_c = 1 - core
    right = {"fsdp": index_of(z_at, x_at + 1, core)}
    left = {"fsdp": index_of(z_at, x_at + 3, core)}
    across = {"fsdp": index_of(other_z, x_at, core)}
    twin = {"fsdp": index_of(z_at, x_at, other_c)}
    peers = [{"fsdp": lax.rem(me + k, seqs)} for k in range(1, seqs)]
    mates = []
    for bit in range(bits):
        gap = 1 << bit
        mates.append({"rep": rep + gap * (1 - 2 * lax.rem(lax.div(rep, gap), 2))})

    used = [0]

    def remote(src, dst, number, device):
        return pltpu.make_async_remote_copy(
            src_ref=src,
            dst_ref=dst,
            send_sem=ssem.at[number],
            recv_sem=rsem.at[number],
            device_id=device,
            device_id_type=MESH,
        )

    started = []

    def send(src, dst, device):
        number = used[0]
        used[0] += 1
        copy = remote(src, dst, number, device)
        copy.start()
        started.append(copy)
        return number

    def landed(dst, number):
        remote(dst, dst, number, twin).wait_recv()

    loads = [
        pltpu.make_async_copy(hid_hbm, hid, local_sem.at[0]),
        pltpu.make_async_copy(val_hbm, val, local_sem.at[1]),
        pltpu.make_async_copy(cot_hbm, cot, local_sem.at[2]),
        pltpu.make_async_copy(own_ref, wts.at[me], local_sem.at[3]),
    ]
    for load in loads:
        load.start()

    barrier = pltpu.get_barrier_semaphore()
    for device in peers + mates:
        pl.semaphore_signal(barrier, inc=1, device_id=device, device_id_type=MESH)
    pl.semaphore_wait(barrier, len(peers) + len(mates))

    top = pl.ds(0, half)
    low = pl.ds(half, half)
    mine = wts.at[me]
    n_across = send(own_ref, mine, across)
    n_right = send(own_ref, mine, right)
    n_left = send(own_ref, mine, left)
    n_twin = [send(own_ref, mine, twin)]

    row_id = lax.broadcasted_iota(jnp.int32, (WIDTH, chunk), 0)

    def fill(h, carry):
        lane = ((row_id & (heads - 1)) == h) & (row_id < 3 * heads)
        rhs[h] = jnp.where(lane, 1.0, 0.0).astype(BF16)
        return carry

    lax.fori_loop(0, heads, fill, 0)

    def spread(z, n_r, n_l):
        at_l = index_of(z, x_at + 3, core)
        at_r = index_of(z, x_at + 1, core)
        landed(wts.at[at_l], n_r)
        f_r = send(wts.at[at_l, top], wts.at[at_l, top], right)
        n_twin.append(send(wts.at[at_l], wts.at[at_l], twin))
        landed(wts.at[at_r], n_l)
        f_l = send(wts.at[at_r, low], wts.at[at_r, low], left)
        n_twin.append(send(wts.at[at_r], wts.at[at_r], twin))
        return f_r, f_l

    def last(z, f_r, f_l):
        at_2 = index_of(z, x_at + 2, core)
        landed(wts.at[at_2, top], f_r)
        landed(wts.at[at_2, low], f_l)
        n_twin.append(send(wts.at[at_2], wts.at[at_2], twin))

    forward = spread(z_at, n_right, n_left)
    at_z = index_of(other_z, x_at, core)
    landed(wts.at[at_z], n_across)
    n_right2 = send(wts.at[at_z], wts.at[at_z], right)
    n_left2 = send(wts.at[at_z], wts.at[at_z], left)
    n_twin.append(send(wts.at[at_z], wts.at[at_z], twin))
    last(z_at, *forward)
    forward = spread(other_z, n_right2, n_left2)
    last(other_z, *forward)
    order = [
        (z_at, 0),
        (z_at, 3),
        (z_at, 1),
        (other_z, 0),
        (z_at, 2),
        (other_z, 3),
        (other_z, 1),
        (other_z, 2),
    ]
    for (z, dx), number in zip(order, n_twin):
        landed(wts.at[index_of(z, x_at + dx, other_c)], number)
    for load in loads:
        load.wait()

    n_part_p = [send(own_ref, part_p.at[bit], mates[bit]) for bit in range(bits)]

    feat[...] = jnp.zeros_like(feat)
    logits = jnp.zeros((heads, chunk), F32)
    for f in range(seqs):
        tokens = hid[:, f * chunk : (f + 1) * chunk]
        feat[...] += nn(tokens, wts[f, :state2, :])
        logits += nt(wts[f, state2:, :], tokens)
    logits = logits + bcol_ref[...]
    small = jnp.exp(-jnp.abs(logits))
    log_part = jnp.where(
        small < 0.01, small * (1.0 - small * (0.5 - small * (1.0 / 3.0))), jnp.log(1.0 + small)
    )
    step = jnp.maximum(logits, 0.0) + log_part
    gate = jnp.where(logits >= 0.0, 1.0, small) / (1.0 + small)
    step_safe = jnp.maximum(step, TINY)
    ratio = jnp.where(logits < -20.0, 1.0, gate / step_safe)
    decay = -jnp.exp(acol_ref[...])
    at_u = lax.broadcasted_iota(jnp.int32, (chunk, chunk), 0)
    at_t = lax.broadcasted_iota(jnp.int32, (chunk, chunk), 1)
    upper = jnp.where(at_u <= at_t, 1.0, 0.0)
    c2 = nn(decay * step, upper, HIGH) * LOG2E
    du = jnp.log2(step_safe) - c2
    parts = split3(du) + (jnp.ones((WIDTH - 3 * heads, chunk), F32),)
    du3[...] = jnp.concatenate(parts, axis=0).T.astype(BF16)
    c_parts = split3(c2)
    for k in range(3):
        rhs[:, 3 * heads + k, :] = c_parts[k].astype(BF16)
    b_proj = feat[:, :WIDTH]
    c_proj = feat[:, WIDTH:]
    allowed = (at_u <= at_t) & (epc_ref[...] == epr_ref[...])
    scores[...] = jnp.where(allowed, nt(b_proj, c_proj, HIGH), 0.0)
    ds0[...] = jnp.zeros_like(ds0)
    ds1[...] = jnp.zeros_like(ds1)
    ones8 = jnp.ones((8, WIDTH), BF16)

    def head_step(h, carry):
        lanes = pl.ds(pl.multiple_of(h * WIDTH, WIDTH), WIDTH)
        xh = val[:, lanes]
        gh = cot[:, lanes]
        rh = rhs[h]
        g0 = nt(xh[:WIDTH], gh)
        g1 = nt(xh[WIDTH:], gh[WIDTH:])
        e0 = jnp.exp2(jnp.minimum(nn(du3[:WIDTH], rh), CAP))
        e1 = jnp.exp2(jnp.minimum(nn(du3[WIDTH:], rh[:, WIDTH:]), CAP))
        ds0[...] += g0 * e0
        ds1[...] += g1 * e1
        v0 = e0 * scores[:WIDTH]
        v1 = e1 * scores[WIDTH:, WIDTH:]
        m0 = jnp.sum((v0 * g0).reshape(WIDTH // 8, 8, -1), axis=0)
        m1 = jnp.sum((v1 * g1).reshape(WIDTH // 8, 8, -1), axis=0)
        mrow[h, :, :WIDTH] = m0[:, :WIDTH]
        mrow[h, :, WIDTH:] = m0[:, WIDTH:] + m1
        dx0 = nn(v0.astype(BF16), gh)
        dx1 = nn(v1.astype(BF16), gh[WIDTH:])
        dx = jnp.concatenate([dx0, dx1], axis=0)
        sgr[:, lanes] = dx.astype(BF16)
        prod = dx * xh.astype(F32)
        high = prod.astype(BF16)
        rest = (prod - high.astype(F32)).astype(BF16)
        col = nt(ones8, high) + nt(ones8, rest)
        mcol[h] = col
        return carry

    lax.fori_loop(0, heads, head_step, 0)
    out_sgr = pltpu.make_async_copy(sgr, sgr_hbm, local_sem.at[4])
    out_sgr.start()

    lower = jnp.where(at_u >= at_t, 1.0, 0.0)
    mc = jnp.sum(mcol[...], axis=1) * 0.125
    drate = nn(jnp.sum(mrow[...], axis=1) - mc, lower, HIGH)
    dlogit = mc * ratio + gate * (decay * drate)
    ddecay = decay * step * drate
    stack = jnp.concatenate(
        [ddecay, dlogit, jnp.zeros((WIDTH - 2 * heads, chunk), F32)], axis=0
    )
    heads_in[me] = nt(jnp.ones((8, chunk), F32), stack, HIGH)
    ds_full = jnp.concatenate(
        [
            ds0[...],
            jnp.concatenate([jnp.zeros((WIDTH, WIDTH), F32), ds1[...]], axis=1),
        ],
        axis=0,
    )
    ds_full = jnp.where(allowed, ds_full, 0.0)
    db = nn(ds_full, c_proj, HIGH)
    dct = nn(b_proj.T, ds_full, HIGH)
    fgt[:WIDTH] = db.T.astype(BF16)
    fgt[WIDTH:state2] = dct.astype(BF16)
    fgt[state2:] = dlogit.astype(BF16)
    fg[:, :WIDTH] = db.astype(BF16)
    fg[:, WIDTH:] = dct.T.astype(BF16)
    wide = jnp.concatenate([dlogit, jnp.zeros((WIDTH - heads, chunk), F32)], axis=0)
    fgl[...] = wide.T.astype(BF16)

    n_heads = [send(heads_in.at[me], heads_in.at[me], device) for device in peers]

    places = [(z, dx) for z in (other_z, z_at) for dx in (2, 1, 3, 0)]

    def columns(index):
        return pl.ds(pl.multiple_of(index * chunk, chunk), chunk)

    n_core = []
    for slot, (z, dx) in enumerate(places):
        index = index_of(z, x_at + dx, other_c)
        dwo[slot] = nn(fgt[...], hid[:, columns(index)]).astype(BF16)
        n_core.append(send(dwo.at[slot], from_core.at[slot], twin))

    def own_part(slot):
        z, dx = places[slot]
        index = index_of(z, x_at + dx, core)
        total = nn(fgt[...], hid[:, columns(index)])
        landed(from_core.at[slot], n_core[slot])
        return total + from_core[slot].astype(F32)

    def layer_part(index):
        spot = columns(index)
        w = wts[index]
        lay[:, spot] = (
            nt(fg[...], w[:state2]) + nn(fgl[:, :heads], w[state2:])
        ).astype(BF16)

    def ring(base, k):
        two = own_part(base)
        acc[base] = two.astype(BF16)
        r1 = send(acc.at[base, top], hop1.at[k, 0], right)
        l1 = send(acc.at[base, low], hop1.at[k, 1], left)
        plus = own_part(base + 1)
        minus = own_part(base + 2)
        acc[base + 1, low] = plus[half:].astype(BF16)
        acc[base + 2, top] = minus[:half].astype(BF16)
        r2 = send(acc.at[base + 1, low], hop2.at[k, 0, low], right)
        l2 = send(acc.at[base + 2, top], hop2.at[k, 1, top], left)
        zero = own_part(base + 3)
        return r1, l1, r2, l2, plus[:half], minus[half:], zero

    def ring_next(base, k, r1, l1, plus, minus):
        landed(hop1.at[k, 0], r1)
        acc[base + 1, top] = (plus + hop1[k, 0].astype(F32)).astype(BF16)
        r3 = send(acc.at[base + 1, top], hop2.at[k, 0, top], right)
        landed(hop1.at[k, 1], l1)
        acc[base + 2, low] = (minus + hop1[k, 1].astype(F32)).astype(BF16)
        l3 = send(acc.at[base + 2, low], hop2.at[k, 1, low], left)
        return r3, l3

    def ring_end(k, r2, l2, r3, l3, zero):
        landed(hop2.at[k, 0, low], r2)
        landed(hop2.at[k, 1, top], l2)
        landed(hop2.at[k, 0, top], r3)
        landed(hop2.at[k, 1, low], l3)
        return zero + hop2[k, 0].astype(F32) + hop2[k, 1].astype(F32)

    r1, l1, r2, l2, plus, minus, zero = ring(0, 0)
    for index in range(0, 4):
        layer_part(index)
    r3, l3 = ring_next(0, 0, r1, l1, plus, minus)
    s1, m1, s2, m2, plus, minus, zero2 = ring(4, 1)
    for index in range(4, 8):
        layer_part(index)
    done = ring_end(0, r2, l2, r3, l3, zero)
    zsend[...] = done.astype(BF16)
    n_z = send(zsend, from_z, across)
    s3, m3 = ring_next(4, 1, s1, m1, plus, minus)
    for index in range(8, seqs):
        layer_part(index)
    out_lay = pltpu.make_async_copy(lay, lay_hbm, local_sem.at[5])
    out_lay.start()
    total = ring_end(1, s2, m2, s3, m3, zero2)
    landed(from_z, n_z)
    grad = total + from_z[...].astype(F32)
    gsend[...] = grad.astype(BF16)
    n_part_g = [send(gsend, part_g.at[bit], mates[bit]) for bit in range(bits)]

    def lanes_sum(value):
        total = jnp.sum(value * value, axis=0, keepdims=True)
        return total[:, :WIDTH] + total[:, WIDTH:]

    state_own = state_ref[...]
    step_own = step_ref[...]
    sums_in[me] = jnp.concatenate(
        [
            lanes_sum(grad[:state2]),
            lanes_sum(grad[state2:]),
            lanes_sum(state_own),
            lanes_sum(step_own),
            jnp.zeros((4, WIDTH), F32),
        ],
        axis=0,
    )
    n_sums = [send(sums_in.at[me], sums_in.at[me], device) for device in peers]

    for k, number in enumerate(n_heads):
        landed(heads_in.at[lax.rem(me + seqs - k - 1, seqs)], number)
    head_grad = jnp.sum(heads_in[...], axis=0)[:1]
    head_own = head_ref[...]
    head_sq = jnp.sum(head_own * head_own, axis=1, keepdims=True) / (2 * heads)
    hgrad_sq = jnp.sum(head_grad * head_grad, axis=1, keepdims=True) / (2 * heads)
    head_trust = jnp.sqrt(head_sq) / jnp.sqrt(hgrad_sq + EPS)
    head_new = head_own - RATE * head_trust * head_grad

    for k, number in enumerate(n_sums):
        landed(sums_in.at[lax.rem(me + seqs - k - 1, seqs)], number)
    squares = jnp.sum(jnp.sum(sums_in[...], axis=0), axis=1, keepdims=True)
    width = seqs * chunk
    state_trust = jnp.sqrt(squares[2:3] / (width * state2)) / jnp.sqrt(
        squares[0:1] / (width * state2) + EPS
    )
    step_trust = jnp.sqrt(squares[3:4] / (width * heads)) / jnp.sqrt(
        squares[1:2] / (width * heads) + EPS
    )
    final = jnp.concatenate(
        [
            head_new,
            jnp.broadcast_to(state_trust, (1, WIDTH)),
            jnp.broadcast_to(step_trust, (1, WIDTH)),
            jnp.zeros((5, WIDTH), F32),
        ],
        axis=0,
    )
    final_send[...] = final
    n_final = [send(final_send, part_s.at[bit], mates[bit]) for bit in range(bits)]
    for bit in range(bits):
        landed(part_p.at[bit], n_part_p[bit])
        landed(part_g.at[bit], n_part_g[bit])
        landed(part_s.at[bit], n_final[bit])
    bit = bit_ref[0]
    mate_p = part_p[bit].astype(F32)
    mate_g = part_g[bit].astype(F32)
    mate_s = part_s[bit]
    move = state_trust * grad[:state2] + mate_s[1:2, :1] * mate_g[:state2]
    nstate_ref[...] = 0.5 * (state_own + mate_p[:state2]) - (0.5 * RATE) * move.T
    move = step_trust * grad[state2:] + mate_s[2:3, :1] * mate_g[state2:]
    nstep_ref[...] = 0.5 * (step_own + mate_p[state2:]) - (0.5 * RATE) * move
    nhead_ref[...] = 0.5 * (final + mate_s)

    out_sgr.wait()
    out_lay.wait()
    for copy in started:
        copy.wait_send()


def count_copies(reps, seqs):
    bits = reps.bit_length() - 1
    return 4 + 2 * 4 + 3 + 2 + 3 * bits + 2 * (seqs - 1) + 8 + 12 + 1


def on_device(
    hidden_in, scan_in, grad_out, episodes, gossip_step, state_proj, step_proj, decay_log, step_bias
):
    reps = lax.axis_size("rep")
    seqs = lax.axis_size("fsdp")
    bits = reps.bit_length() - 1
    chosen = gossip_step % bits
    state_own = state_proj[0]
    step_own = step_proj[0]
    own = jnp.concatenate([state_own, step_own], axis=0).astype(BF16)
    heads = step_own.shape[0]
    length, inner = scan_in.shape[2:]
    model = hidden_in.shape[3]
    chunk = model // seqs
    rows = own.shape[0]
    state2 = 2 * WIDTH
    episode = episodes[0, 0]
    head_row = jnp.concatenate(
        [decay_log[0], step_bias[0], jnp.zeros((WIDTH - 2 * heads,), F32)]
    ).reshape(1, WIDTH)
    half = rows // 2
    vmem = pl.BlockSpec(memory_space=pltpu.VMEM)
    anyspace = pl.BlockSpec(memory_space=pl.ANY)
    copies = count_copies(reps, seqs) + 8
    outs = pl.pallas_call(
        functools.partial(layer_kernel, (heads, reps, seqs, chunk, rows)),
        out_shape=(
            jax.ShapeDtypeStruct((length, model), BF16),
            jax.ShapeDtypeStruct((length, inner), BF16),
            jax.ShapeDtypeStruct((chunk, state2), F32),
            jax.ShapeDtypeStruct((heads, chunk), F32),
            jax.ShapeDtypeStruct((8, WIDTH), F32),
        ),
        in_specs=[pl.BlockSpec(memory_space=pltpu.SMEM), vmem, vmem, vmem]
        + [anyspace] * 3
        + [vmem] * 5,
        out_specs=(anyspace, anyspace, vmem, vmem, vmem),
        scratch_shapes=[
            pltpu.VMEM((length, model), BF16),
            pltpu.VMEM((length, inner), BF16),
            pltpu.VMEM((length, inner), BF16),
            pltpu.VMEM((seqs, rows, chunk), BF16),
            pltpu.VMEM((8, rows, chunk), BF16),
            pltpu.VMEM((8, rows, chunk), BF16),
            pltpu.VMEM((8, rows, chunk), BF16),
            pltpu.VMEM((2, 2, half, chunk), BF16),
            pltpu.VMEM((2, 2, rows, chunk), BF16),
            pltpu.VMEM((rows, chunk), BF16),
            pltpu.VMEM((bits, rows, chunk), BF16),
            pltpu.VMEM((bits, rows, chunk), BF16),
            pltpu.VMEM((bits, 8, WIDTH), F32),
            pltpu.VMEM((rows, chunk), BF16),
            pltpu.VMEM((rows, chunk), BF16),
            pltpu.VMEM((seqs, 8, WIDTH), F32),
            pltpu.VMEM((seqs, 8, WIDTH), F32),
            pltpu.VMEM((8, WIDTH), F32),
            pltpu.VMEM((length, model), BF16),
            pltpu.VMEM((length, inner), BF16),
            pltpu.VMEM((length, state2), F32),
            pltpu.VMEM((length, WIDTH), BF16),
            pltpu.VMEM((heads, WIDTH, length), BF16),
            pltpu.VMEM((length, length), F32),
            pltpu.VMEM((WIDTH, length), F32),
            pltpu.VMEM((WIDTH, WIDTH), F32),
            pltpu.VMEM((heads, 8, length), F32),
            pltpu.VMEM((heads, 8, length), F32),
            pltpu.VMEM((rows, length), BF16),
            pltpu.VMEM((length, state2), BF16),
            pltpu.VMEM((length, WIDTH), BF16),
            pltpu.SemaphoreType.DMA((6,)),
            pltpu.SemaphoreType.DMA((copies,)),
            pltpu.SemaphoreType.DMA((copies,)),
        ],
        compiler_params=pltpu.CompilerParams(
            collective_id=0, has_side_effects=True, vmem_limit_bytes=60 * 1024 * 1024
        ),
    )(
        chosen.astype(jnp.int32),
        own,
        state_own,
        step_own,
        hidden_in[0, 0],
        scan_in[0, 0],
        grad_out[0, 0],
        episode[:, None],
        episode[None, :],
        decay_log[0][:, None],
        step_bias[0][:, None],
        head_row,
    )
    layer_grad, scan_grad, new_state, new_step, new_head = outs
    return (
        layer_grad[None, None],
        scan_grad[None, None],
        new_state[None],
        new_step[None],
        new_head[:1, :heads],
        new_head[:1, heads : 2 * heads],
    )


def solution(mesh):
    in_specs = (
        P("rep", "fsdp", None, None),
        P("rep", "fsdp", None, None),
        P("rep", "fsdp", None, None),
        P("rep", "fsdp", None),
        P(),
        P("rep", "fsdp", None),
        P("rep", None, "fsdp"),
        P("rep", None),
        P("rep", None),
    )
    out_specs = (
        P("rep", "fsdp", None, None),
        P("rep", "fsdp", None, None),
        P("rep", "fsdp", None),
        P("rep", None, "fsdp"),
        P("rep", None),
        P("rep", None),
    )
    return jax.shard_map(
        on_device, mesh=mesh, in_specs=in_specs, out_specs=out_specs, check_vma=False
    )
```

```python
import functools

import jax
import jax.numpy as jnp
from jax import lax
from jax.experimental import pallas as pl
from jax.experimental.pallas import tpu as pltpu
from jax.sharding import PartitionSpec as P

MESH = pl.DeviceIdType.MESH
F32 = jnp.float32
BF16 = jnp.bfloat16
HIGH = lax.Precision.HIGHEST
LOG2E = 1.4426950408889634
TINY = 1e-37
CAP = 60.0
RATE = 0.1
EPS = 1e-6
WIDTH = 128
UNROLL = 2
BARRIER_NEAR = True


def nn(a, b, precision=None):
    return lax.dot_general(
        a, b, (((1,), (0,)), ((), ())), precision=precision, preferred_element_type=F32
    )


def nt(a, b, precision=None):
    return lax.dot_general(
        a, b, (((1,), (1,)), ((), ())), precision=precision, preferred_element_type=F32
    )


def split3(value):
    high = value.astype(BF16).astype(F32)
    rest = value - high
    mid = rest.astype(BF16).astype(F32)
    return high, mid, rest - mid


def split2(value):
    high = value.astype(BF16)
    return high, (value - high.astype(F32)).astype(BF16)


def triple(product, a, b):
    ah, al = split2(a)
    bh, bl = split2(b)
    return product(ah, bh) + (product(ah, bl) + product(al, bh))


def exact(product, parts, b):
    high, mid, low = (part.astype(BF16) for part in parts)
    return product(high, b) + (product(mid, b) + product(low, b))


def layer_kernel(
    dims,
    state_ref,
    step_ref,
    ep_ref,
    decay_ref,
    bias_ref,
    hid_hbm,
    val_hbm,
    cot_hbm,
    lay_hbm,
    sgr_hbm,
    nstate_ref,
    nstep_ref,
    ndecay_ref,
    nbias_ref,
    hid,
    val,
    cot,
    wts,
    gmat,
    dwo,
    acc,
    from_core,
    hop1,
    hop2,
    from_z,
    part_p,
    part_g,
    part_s,
    zsend,
    gsend,
    zero_sum,
    keep,
    heads_in,
    sums_in,
    final_send,
    head_own_s,
    lay,
    sgr,
    feat,
    logit_s,
    mask_s,
    du3,
    rhs,
    scores,
    ds0,
    ds1,
    mrow,
    mcol,
    fgt,
    fg,
    fgl,
    local_sem,
    ssem,
    rsem,
):
    heads, seqs, chunk, rows, bit = dims
    half = rows // 2
    state2 = 2 * WIDTH
    me = lax.axis_index("fsdp")
    rep = lax.axis_index("rep")
    core = lax.rem(me, 2)
    x_at = lax.rem(lax.div(me, 2), 4)
    z_at = lax.div(me, 8)

    def index_of(z, x, c):
        return z * 8 + lax.rem(x, 4) * 2 + c

    other_z = 1 - z_at
    other_c = 1 - core
    right = {"fsdp": index_of(z_at, x_at + 1, core)}
    left = {"fsdp": index_of(z_at, x_at + 3, core)}
    across = {"fsdp": index_of(other_z, x_at, core)}
    twin = {"fsdp": index_of(z_at, x_at, other_c)}
    peers = [{"fsdp": lax.rem(me + k, seqs)} for k in range(1, seqs)]
    gap = 1 << bit
    mate = {"rep": rep + gap * (1 - 2 * lax.rem(lax.div(rep, gap), 2))}

    used = [0]
    started = []

    def remote(src, dst, number, device):
        return pltpu.make_async_remote_copy(
            src_ref=src,
            dst_ref=dst,
            send_sem=ssem.at[number],
            recv_sem=rsem.at[number],
            device_id=device,
            device_id_type=MESH,
        )

    def send(src, dst, device):
        number = used[0]
        used[0] += 1
        copy = remote(src, dst, number, device)
        copy.start()
        started.append(copy)
        return number

    def landed(dst, number):
        remote(dst, dst, number, twin).wait_recv()

    barrier = pltpu.get_barrier_semaphore()
    near = (twin, right, left, across, mate) if BARRIER_NEAR else peers + [mate]
    for device in near:
        pl.semaphore_signal(barrier, inc=1, device_id=device, device_id_type=MESH)
    loads = [
        pltpu.make_async_copy(val_hbm, val, local_sem.at[0]),
        pltpu.make_async_copy(cot_hbm, cot, local_sem.at[1]),
        pltpu.make_async_copy(hid_hbm, hid, local_sem.at[2]),
    ]
    for load in loads:
        load.start()

    wts[me, :state2] = state_ref[...].astype(BF16)
    wts[me, state2:] = step_ref[...].astype(BF16)
    at_u = lax.broadcasted_iota(jnp.int32, (chunk, chunk), 0)
    at_t = lax.broadcasted_iota(jnp.int32, (chunk, chunk), 1)
    ep_t = jnp.broadcast_to(ep_ref[...].astype(F32), (chunk, chunk))
    mask_s[...] = jnp.where((at_u <= at_t) & (ep_t.T == ep_t), 1.0, 0.0)
    eye_r = lax.broadcasted_iota(jnp.int32, (heads, heads), 0)
    eye_c = lax.broadcasted_iota(jnp.int32, (heads, heads), 1)

    def column(row_ref):
        spread_row = jnp.broadcast_to(row_ref[...], (heads, heads))
        return jnp.sum(jnp.where(eye_r == eye_c, spread_row, 0.0), axis=1, keepdims=True)

    decay = -jnp.exp(column(decay_ref))
    bias_col = column(bias_ref)
    place_r = lax.broadcasted_iota(jnp.int32, (heads, WIDTH), 0)
    place_c = lax.broadcasted_iota(jnp.int32, (heads, WIDTH), 1)
    place_d = jnp.where(place_c == place_r, 1.0, 0.0)
    place_b = jnp.where(place_c == place_r + heads, 1.0, 0.0)
    head_own_s[...] = nn(jnp.broadcast_to(decay_ref[...], (8, heads)), place_d, HIGH) + nn(
        jnp.broadcast_to(bias_ref[...], (8, heads)), place_b, HIGH
    )
    feat[...] = jnp.zeros_like(feat)
    logit_s[...] = jnp.zeros_like(logit_s)
    ds0[...] = jnp.zeros_like(ds0)
    ds1[...] = jnp.zeros_like(ds1)
    pl.semaphore_wait(barrier, len(near))

    top = pl.ds(0, half)
    low = pl.ds(half, half)
    halves = (top, low)

    def pass_on(index, part, device):
        return send(wts.at[index, part], wts.at[index, part], device)

    n_across = [pass_on(me, part, across) for part in halves]
    n_rt = pass_on(me, top, right)
    n_ll = pass_on(me, low, left)
    n_rl = pass_on(me, low, right)
    n_lt = pass_on(me, top, left)

    def share(index):
        return send(wts.at[index], wts.at[index], twin)

    n_own = share(me)

    row_id = lax.broadcasted_iota(jnp.int32, (WIDTH, chunk), 0)
    loads[0].wait()
    loads[1].wait()

    def prepare(pair, carry):
        for k in range(2):
            h = pair * 2 + k
            lane = ((row_id & (heads - 1)) == h) & (row_id < 3 * heads)
            rhs[h] = jnp.where(lane, 1.0, 0.0).astype(BF16)
            lanes = pl.ds(pl.multiple_of(h * WIDTH, WIDTH), WIDTH)
            xh = val[:, lanes]
            gh = cot[:, lanes]
            gmat[h, :WIDTH] = nt(xh[:WIDTH], gh)
            gmat[h, WIDTH:, WIDTH:] = nt(xh[WIDTH:], gh[WIDTH:])
        return carry

    lax.fori_loop(0, heads // 2, prepare, 0)
    loads[2].wait()

    def columns(index):
        return pl.ds(pl.multiple_of(index * chunk, chunk), chunk)

    def feat_part(index):
        tokens = hid[:, columns(index)]
        feat[...] += nn(tokens, wts[index, :state2, :])
        logit_s[:, :heads] += nt(tokens, wts[index, state2:, :])

    def spread(z, n_rt, n_rl, n_ll, n_lt):
        at_l = index_of(z, x_at + 3, core)
        at_r = index_of(z, x_at + 1, core)
        landed(wts.at[at_l, top], n_rt)
        f_r = pass_on(at_l, top, right)
        landed(wts.at[at_r, low], n_ll)
        f_l = pass_on(at_r, low, left)
        landed(wts.at[at_l, low], n_rl)
        t_l = share(at_l)
        landed(wts.at[at_r, top], n_lt)
        t_r = share(at_r)
        return at_l, at_r, f_r, f_l, t_l, t_r

    def shared(z, dx, number):
        index = index_of(z, x_at + dx, other_c)
        landed(wts.at[index], number)
        feat_part(index)

    at_l, at_r, f_r, f_l, t_l, t_r = spread(z_at, n_rt, n_rl, n_ll, n_lt)
    feat_part(me)
    shared(z_at, 0, n_own)
    at_z = index_of(other_z, x_at, core)
    landed(wts.at[at_z, top], n_across[0])
    z_rt = pass_on(at_z, top, right)
    feat_part(at_l)
    landed(wts.at[at_z, low], n_across[1])
    z_ll = pass_on(at_z, low, left)
    z_rl = pass_on(at_z, low, right)
    z_lt = pass_on(at_z, top, left)
    t_z = share(at_z)
    at_2 = index_of(z_at, x_at + 2, core)
    landed(wts.at[at_2, top], f_r)
    landed(wts.at[at_2, low], f_l)
    t_2 = share(at_2)
    feat_part(at_r)
    feat_part(at_z)
    feat_part(at_2)
    shared(z_at, 3, t_l)
    shared(z_at, 1, t_r)
    shared(other_z, 0, t_z)
    shared(z_at, 2, t_2)
    at_l, at_r, f_r, f_l, t_l, t_r = spread(other_z, z_rt, z_rl, z_ll, z_lt)
    feat_part(at_l)
    feat_part(at_r)
    shared(other_z, 3, t_l)
    shared(other_z, 1, t_r)
    at_2 = index_of(other_z, x_at + 2, core)
    landed(wts.at[at_2, top], f_r)
    t_2t = pass_on(at_2, top, twin)
    landed(wts.at[at_2, low], f_l)
    t_2l = pass_on(at_2, low, twin)
    feat_part(at_2)
    at_2 = index_of(other_z, x_at + 2, other_c)
    landed(wts.at[at_2, top], t_2t)
    landed(wts.at[at_2, low], t_2l)
    feat_part(at_2)

    n_part_p = send(wts.at[me], part_p, mate)

    logits = logit_s[...].T[:heads] + bias_col
    small = jnp.exp(-jnp.abs(logits))
    log_part = jnp.where(
        small < 0.01, small * (1.0 - small * (0.5 - small * (1.0 / 3.0))), jnp.log(1.0 + small)
    )
    step = jnp.maximum(logits, 0.0) + log_part
    gate = jnp.where(logits >= 0.0, 1.0, small) / (1.0 + small)
    step_safe = jnp.maximum(step, TINY)
    ratio = jnp.where(logits < -20.0, 1.0, gate / step_safe)
    upper = jnp.where(at_u <= at_t, 1.0, 0.0).astype(BF16)
    c2 = exact(nn, split3(decay * step), upper) * LOG2E
    du = jnp.log2(step_safe) - c2
    parts = split3(du) + (jnp.ones((WIDTH - 3 * heads, chunk), F32),)
    du3[...] = jnp.concatenate(parts, axis=0).T.astype(BF16)
    c_parts = split3(c2)
    for k in range(3):
        rhs[:, 3 * heads + k, :] = c_parts[k].astype(BF16)
    b_proj = feat[:, :WIDTH]
    c_proj = feat[:, WIDTH:]
    scores[...] = jnp.where(mask_s[...] > 0.5, triple(nt, b_proj, c_proj), 0.0)
    ones8 = jnp.ones((8, WIDTH), BF16)

    def head_group(group, carry):
        p0 = 0.0
        p1 = 0.0
        for k in range(UNROLL):
            h = group * UNROLL + k
            lanes = pl.ds(pl.multiple_of(h * WIDTH, WIDTH), WIDTH)
            gh = cot[:, lanes]
            rh = rhs[h]
            g0 = gmat[h, :WIDTH]
            g1 = gmat[h, WIDTH:, WIDTH:]
            e0 = jnp.exp2(jnp.minimum(nn(du3[:WIDTH], rh), CAP))
            e1 = jnp.exp2(jnp.minimum(nn(du3[WIDTH:], rh[:, WIDTH:]), CAP))
            p0 = p0 + g0 * e0
            p1 = p1 + g1 * e1
            v0 = e0 * scores[:WIDTH]
            v1 = e1 * scores[WIDTH:, WIDTH:]
            v0 = v0.astype(BF16)
            v1 = v1.astype(BF16)
            m0 = jnp.sum((v0.astype(F32) * g0).reshape(WIDTH // 8, 8, -1), axis=0)
            m1 = jnp.sum((v1.astype(F32) * g1).reshape(WIDTH // 8, 8, -1), axis=0)
            mrow[h, :, :WIDTH] = m0[:, :WIDTH]
            mrow[h, :, WIDTH:] = m0[:, WIDTH:] + m1
            dx0 = nn(v0, gh)
            dx1 = nn(v1, gh[WIDTH:])
            dx = jnp.concatenate([dx0, dx1], axis=0)
            sgr[:, lanes] = dx.astype(BF16)
            high, rest = split2(dx * val[:, lanes].astype(F32))
            mcol[h] = nt(ones8, high) + nt(ones8, rest)
        ds0[...] += p0
        ds1[...] += p1
        return carry

    lax.fori_loop(0, heads // UNROLL, head_group, 0)
    out_sgr = pltpu.make_async_copy(sgr, sgr_hbm, local_sem.at[4])
    out_sgr.start()

    lower = jnp.where(at_u >= at_t, 1.0, 0.0).astype(BF16)
    mc = jnp.sum(mcol[...], axis=1) * 0.125
    drate = exact(nn, split3(jnp.sum(mrow[...], axis=1) - mc), lower)
    dlogit = mc * ratio + gate * (decay * drate)
    ddecay = decay * step * drate
    stack = jnp.concatenate(
        [ddecay, dlogit, jnp.zeros((WIDTH - 2 * heads, chunk), F32)], axis=0
    )
    ds_full = jnp.concatenate(
        [
            ds0[...],
            jnp.concatenate([jnp.zeros((WIDTH, WIDTH), F32), ds1[...]], axis=1),
        ],
        axis=0,
    )
    ds_full = jnp.where(mask_s[...] > 0.5, ds_full, 0.0)
    db = triple(nn, ds_full, c_proj)
    dct = triple(nn, b_proj.T, ds_full)
    fgt[:WIDTH] = db.T.astype(BF16)
    fgt[WIDTH:state2] = dct.astype(BF16)
    fgt[state2:] = dlogit.astype(BF16)

    places = [(z, dx) for z in (other_z, z_at) for dx in (2, 1, 3, 0)]
    n_core = {}

    def twin_part(slot):
        z, dx = places[slot]
        index = index_of(z, x_at + dx, other_c)
        dwo[slot] = nn(fgt[...], hid[:, columns(index)]).astype(BF16)
        n_core[slot] = send(dwo.at[slot], from_core.at[slot], twin)

    def own_part(slot):
        z, dx = places[slot]
        index = index_of(z, x_at + dx, core)
        total = nn(fgt[...], hid[:, columns(index)])
        landed(from_core.at[slot], n_core[slot])
        return total + from_core[slot].astype(F32)

    def layer_part(index):
        spot = columns(index)
        w = wts[index]
        lay[:, spot] = (
            nt(fg[...], w[:state2]) + nn(fgl[:, :heads], w[state2:])
        ).astype(BF16)

    def ring_first(base, k):
        twin_part(base)
        twin_part(base + 1)
        acc[base] = own_part(base).astype(BF16)
        r1 = send(acc.at[base, top], hop1.at[k, 0], right)
        l1 = send(acc.at[base, low], hop1.at[k, 1], left)
        twin_part(base + 2)
        plus = own_part(base + 1)
        acc[base + 1, low] = plus[half:].astype(BF16)
        keep[k, 0] = plus[:half]
        r2 = send(acc.at[base + 1, low], hop2.at[k, 0, low], right)
        twin_part(base + 3)
        minus = own_part(base + 2)
        acc[base + 2, top] = minus[:half].astype(BF16)
        keep[k, 1] = minus[half:]
        l2 = send(acc.at[base + 2, top], hop2.at[k, 1, top], left)
        return r1, l1, r2, l2

    def ring_next(base, k, r1, l1):
        landed(hop1.at[k, 0], r1)
        acc[base + 1, top] = (keep[k, 0] + hop1[k, 0].astype(F32)).astype(BF16)
        r3 = send(acc.at[base + 1, top], hop2.at[k, 0, top], right)
        landed(hop1.at[k, 1], l1)
        acc[base + 2, low] = (keep[k, 1] + hop1[k, 1].astype(F32)).astype(BF16)
        l3 = send(acc.at[base + 2, low], hop2.at[k, 1, low], left)
        zero_sum[k] = own_part(base + 3)
        return r3, l3

    def ring_end(k, part, first, second):
        landed(hop2.at[k, 0, part], first)
        landed(hop2.at[k, 1, part], second)
        return (
            zero_sum[k, part, :]
            + hop2[k, 0, part, :].astype(F32)
            + hop2[k, 1, part, :].astype(F32)
        )

    r1, l1, r2, l2 = ring_first(0, 0)
    r3, l3 = ring_next(0, 0, r1, l1)
    s1, m1, s2, m2 = ring_first(4, 1)
    zsend[top, :] = ring_end(0, top, r3, l2).astype(BF16)
    n_z = [send(zsend.at[top], from_z.at[top], across)]
    zsend[low, :] = ring_end(0, low, r2, l3).astype(BF16)
    n_z.append(send(zsend.at[low], from_z.at[low], across))
    s3, m3 = ring_next(4, 1, s1, m1)

    sums8 = exact(lambda a, b: nt(b, a), split3(stack), jnp.ones((8, chunk), BF16))
    heads_in[me] = sums8
    n_heads = [send(heads_in.at[me], heads_in.at[me], device) for device in peers]
    fg[:, :WIDTH] = db.astype(BF16)
    fg[:, WIDTH:] = dct.T.astype(BF16)
    wide = jnp.concatenate([dlogit, jnp.zeros((WIDTH - heads, chunk), F32)], axis=0)
    fgl[...] = wide.T.astype(BF16)
    for index in range(seqs):
        layer_part(index)
    out_lay = pltpu.make_async_copy(lay, lay_hbm, local_sem.at[5])
    out_lay.start()

    for k, number in enumerate(n_heads):
        landed(heads_in.at[lax.rem(me + seqs - k - 1, seqs)], number)
    head_grad = jnp.sum(heads_in[...], axis=0)[:1]
    head_own = head_own_s[:1]
    head_sq = jnp.sum(head_own * head_own, axis=1, keepdims=True) / (2 * heads)
    hgrad_sq = jnp.sum(head_grad * head_grad, axis=1, keepdims=True) / (2 * heads)
    head_trust = jnp.sqrt(head_sq) / jnp.sqrt(hgrad_sq + EPS)
    final_send[:1] = head_own - RATE * head_trust * head_grad

    def lanes_sum(value):
        total = jnp.sum(value * value, axis=0, keepdims=True)
        return total[:, :WIDTH] + total[:, WIDTH:]

    state_own = state_ref[...]
    step_own = step_ref[...]
    own_sq = [lanes_sum(state_own), lanes_sum(step_own)]

    total_t = ring_end(1, top, s3, m2)
    total_l = ring_end(1, low, s2, m3)
    landed(from_z.at[top], n_z[0])
    grad_t = total_t + from_z[top, :].astype(F32)
    gsend[top, :] = grad_t.astype(BF16)
    n_part_g = [send(gsend.at[top], part_g.at[top], mate)]
    landed(from_z.at[low], n_z[1])
    grad_l = total_l + from_z[low, :].astype(F32)
    gsend[low, :] = grad_l.astype(BF16)
    n_part_g.append(send(gsend.at[low], part_g.at[low], mate))
    grad = jnp.concatenate([grad_t, grad_l], axis=0)

    sums_in[me] = jnp.concatenate(
        [lanes_sum(grad[:state2]), lanes_sum(grad[state2:])]
        + own_sq
        + [jnp.zeros((4, WIDTH), F32)],
        axis=0,
    )
    n_sums = [send(sums_in.at[me], sums_in.at[me], device) for device in peers]
    for k, number in enumerate(n_sums):
        landed(sums_in.at[lax.rem(me + seqs - k - 1, seqs)], number)
    squares = jnp.sum(jnp.sum(sums_in[...], axis=0), axis=1, keepdims=True)
    width = seqs * chunk
    state_trust = jnp.sqrt(squares[2:3] / (width * state2)) / jnp.sqrt(
        squares[0:1] / (width * state2) + EPS
    )
    step_trust = jnp.sqrt(squares[3:4] / (width * heads)) / jnp.sqrt(
        squares[1:2] / (width * heads) + EPS
    )
    final_send[1:2] = jnp.broadcast_to(state_trust, (1, WIDTH))
    final_send[2:3] = jnp.broadcast_to(step_trust, (1, WIDTH))
    n_final = send(final_send, part_s, mate)
    landed(part_p, n_part_p)
    landed(part_g.at[top], n_part_g[0])
    landed(part_g.at[low], n_part_g[1])
    mate_p = part_p[...].astype(F32)
    mate_g = part_g[...].astype(F32)
    base_state = 0.5 * (state_own + mate_p[:state2]) - (0.5 * RATE) * (
        state_trust * grad[:state2].T
    )
    base_step = 0.5 * (step_own + mate_p[state2:]) - (0.5 * RATE) * (step_trust * grad[state2:])
    mate_state = (0.5 * RATE) * mate_g[:state2].T
    mate_step = (0.5 * RATE) * mate_g[state2:]
    landed(part_s, n_final)
    mate_s = part_s[...]
    nstate_ref[...] = base_state - mate_s[1:2, :1] * mate_state
    nstep_ref[...] = base_step - mate_s[2:3, :1] * mate_step
    head_mix = 0.5 * (final_send[:1] + mate_s[:1])
    ndecay_ref[...] = head_mix[:, :heads]
    nbias_ref[...] = head_mix[:, heads : 2 * heads]

    out_sgr.wait()
    out_lay.wait()
    for copy in started:
        copy.wait_send()


def place_kernel(*refs):
    count = (len(refs) - 1) // 2
    sem = refs[-1]
    copies = [
        pltpu.make_async_copy(refs[k], refs[count + k], sem.at[k]) for k in range(count)
    ]
    for copy in copies:
        copy.start()
    for copy in copies:
        copy.wait()


def on_device(
    hidden_in, scan_in, grad_out, episodes, gossip_step, state_proj, step_proj, decay_log, step_bias
):
    reps = lax.axis_size("rep")
    seqs = lax.axis_size("fsdp")
    bits = reps.bit_length() - 1
    heads = step_proj.shape[1]
    length, inner = scan_in.shape[2:]
    model = hidden_in.shape[3]
    chunk = model // seqs
    state2 = 2 * WIDTH
    rows = state2 + heads
    half = rows // 2
    vmem = pl.BlockSpec(memory_space=pltpu.VMEM)
    anyspace = pl.BlockSpec(memory_space=pl.ANY)
    copies = 100
    shapes = (
        jax.ShapeDtypeStruct((length, model), BF16),
        jax.ShapeDtypeStruct((length, inner), BF16),
        jax.ShapeDtypeStruct((chunk, state2), F32),
        jax.ShapeDtypeStruct((heads, chunk), F32),
        jax.ShapeDtypeStruct((1, heads), F32),
        jax.ShapeDtypeStruct((1, heads), F32),
    )

    def run(bit, *operands):
        outs = pl.pallas_call(
            functools.partial(layer_kernel, (heads, seqs, chunk, rows, bit)),
            out_shape=shapes,
            in_specs=[vmem] * 5 + [anyspace] * 3,
            out_specs=(anyspace, anyspace, vmem, vmem, vmem, vmem),
            scratch_shapes=[
                pltpu.VMEM((length, model), BF16),
                pltpu.VMEM((length, inner), BF16),
                pltpu.VMEM((length, inner), BF16),
                pltpu.VMEM((seqs, rows, chunk), BF16),
                pltpu.VMEM((heads, length, length), F32),
                pltpu.VMEM((8, rows, chunk), BF16),
                pltpu.VMEM((8, rows, chunk), BF16),
                pltpu.VMEM((8, rows, chunk), BF16),
                pltpu.VMEM((2, 2, half, chunk), BF16),
                pltpu.VMEM((2, 2, rows, chunk), BF16),
                pltpu.VMEM((rows, chunk), BF16),
                pltpu.VMEM((rows, chunk), BF16),
                pltpu.VMEM((rows, chunk), BF16),
                pltpu.VMEM((8, WIDTH), F32),
                pltpu.VMEM((rows, chunk), BF16),
                pltpu.VMEM((rows, chunk), BF16),
                pltpu.VMEM((2, rows, chunk), F32),
                pltpu.VMEM((2, 2, half, chunk), F32),
                pltpu.VMEM((seqs, 8, WIDTH), F32),
                pltpu.VMEM((seqs, 8, WIDTH), F32),
                pltpu.VMEM((8, WIDTH), F32),
                pltpu.VMEM((8, WIDTH), F32),
                pltpu.VMEM((length, model), BF16),
                pltpu.VMEM((length, inner), BF16),
                pltpu.VMEM((length, state2), F32),
                pltpu.VMEM((length, WIDTH), F32),
                pltpu.VMEM((length, length), F32),
                pltpu.VMEM((length, WIDTH), BF16),
                pltpu.VMEM((heads, WIDTH, length), BF16),
                pltpu.VMEM((length, length), F32),
                pltpu.VMEM((WIDTH, length), F32),
                pltpu.VMEM((WIDTH, WIDTH), F32),
                pltpu.VMEM((heads, 8, length), F32),
                pltpu.VMEM((heads, 8, length), F32),
                pltpu.VMEM((rows, length), BF16),
                pltpu.VMEM((length, state2), BF16),
                pltpu.VMEM((length, WIDTH), BF16),
                pltpu.SemaphoreType.DMA((6,)),
                pltpu.SemaphoreType.DMA((copies,)),
                pltpu.SemaphoreType.DMA((copies,)),
            ],
            compiler_params=pltpu.CompilerParams(
                collective_id=bit, has_side_effects=True, vmem_limit_bytes=38 * 1024 * 1024
            ),
        )(*operands)
        return tuple(
            pl.pallas_call(
                place_kernel,
                out_shape=shapes,
                in_specs=[anyspace] * len(shapes),
                out_specs=(anyspace,) * len(shapes),
                scratch_shapes=[pltpu.SemaphoreType.DMA((len(shapes),))],
                compiler_params=pltpu.CompilerParams(vmem_limit_bytes=1024 * 1024),
            )(*outs)
        )

    operands = (
        state_proj[0],
        step_proj[0],
        episodes[0],
        decay_log,
        step_bias,
        hidden_in[0, 0],
        scan_in[0, 0],
        grad_out[0, 0],
    )
    outs = lax.switch(
        lax.rem(gossip_step[0], bits), [functools.partial(run, bit) for bit in range(bits)], *operands
    )
    layer_grad, scan_grad, new_state, new_step, new_decay, new_bias = outs
    return (
        layer_grad[None, None],
        scan_grad[None, None],
        new_state[None],
        new_step[None],
        new_decay,
        new_bias,
    )


def solution(mesh):
    in_specs = (
        P("rep", "fsdp", None, None),
        P("rep", "fsdp", None, None),
        P("rep", "fsdp", None, None),
        P("rep", "fsdp", None),
        P(),
        P("rep", "fsdp", None),
        P("rep", None, "fsdp"),
        P("rep", None),
        P("rep", None),
    )
    out_specs = (
        P("rep", "fsdp", None, None),
        P("rep", "fsdp", None, None),
        P("rep", "fsdp", None),
        P("rep", None, "fsdp"),
        P("rep", None),
        P("rep", None),
    )
    return jax.shard_map(
        on_device, mesh=mesh, in_specs=in_specs, out_specs=out_specs, check_vma=False
    )
```

```python
import functools

import jax
import jax.numpy as jnp
from jax import lax
from jax.experimental import pallas as pl
from jax.experimental.pallas import tpu as pltpu
from jax.sharding import PartitionSpec as P

MESH = pl.DeviceIdType.MESH
F32 = jnp.float32
BF16 = jnp.bfloat16
HIGH = lax.Precision.HIGHEST
LOG2E = 1.4426950408889634
TINY = 1e-37
CAP = 60.0
RATE = 0.1
EPS = 1e-6
WIDTH = 128
BARRIER_NEAR = True


def nn(a, b, precision=None):
    return lax.dot_general(
        a, b, (((1,), (0,)), ((), ())), precision=precision, preferred_element_type=F32
    )


def nt(a, b, precision=None):
    return lax.dot_general(
        a, b, (((1,), (1,)), ((), ())), precision=precision, preferred_element_type=F32
    )


def split3(value):
    high = value.astype(BF16).astype(F32)
    rest = value - high
    mid = rest.astype(BF16).astype(F32)
    return high, mid, rest - mid


def split2(value):
    high = value.astype(BF16)
    return high, (value - high.astype(F32)).astype(BF16)


def triple(product, a, b):
    ah, al = split2(a)
    bh, bl = split2(b)
    return product(ah, bh) + (product(ah, bl) + product(al, bh))


def exact(product, parts, b):
    high, mid, low = (part.astype(BF16) for part in parts)
    return product(high, b) + (product(mid, b) + product(low, b))


def layer_kernel(
    dims,
    state_ref,
    step_ref,
    ep_ref,
    decay_ref,
    bias_ref,
    hid_hbm,
    val_hbm,
    cot_hbm,
    lay_hbm,
    sgr_hbm,
    nstate_ref,
    nstep_ref,
    ndecay_ref,
    nbias_ref,
    hid,
    val,
    cot,
    wts,
    gmat,
    dwo,
    acc,
    from_core,
    hop1,
    direct,
    hop2,
    from_z,
    part_p,
    part_g,
    part_s,
    mate_sums,
    zsend,
    gsend,
    grad_s,
    zero_sum,
    keep,
    heads_in,
    sums_in,
    final_send,
    head_own_s,
    lay,
    sgr,
    feat,
    logit_s,
    mask_s,
    du_s,
    c2_s,
    scores,
    ds,
    vbuf,
    mbuf,
    mrow,
    mcol,
    fgt,
    fg,
    fgl,
    local_sem,
    ssem,
    rsem,
):
    heads, seqs, chunk, rows, bit = dims
    half = rows // 2
    state2 = 2 * WIDTH
    me = lax.axis_index("fsdp")
    rep = lax.axis_index("rep")
    core = lax.rem(me, 2)
    x_at = lax.rem(lax.div(me, 2), 4)
    z_at = lax.div(me, 8)

    def index_of(z, x, c):
        return z * 8 + lax.rem(x, 4) * 2 + c

    other_z = 1 - z_at
    other_c = 1 - core
    right = {"fsdp": index_of(z_at, x_at + 1, core)}
    left = {"fsdp": index_of(z_at, x_at + 3, core)}
    across = {"fsdp": index_of(other_z, x_at, core)}
    twin = {"fsdp": index_of(z_at, x_at, other_c)}
    ahead = 1 + 2 * core
    behind = 3 - 2 * core
    fwd = {"fsdp": index_of(z_at, x_at + ahead, core)}
    back = {"fsdp": index_of(z_at, x_at + behind, core)}
    opposite = {"fsdp": index_of(z_at, x_at + 2, core)}
    peers = [{"fsdp": lax.rem(me + k, seqs)} for k in range(1, seqs)]
    gap = 1 << bit
    mate = {"rep": rep + gap * (1 - 2 * lax.rem(lax.div(rep, gap), 2))}

    used = [0]
    started = []

    def remote(src, dst, number, device):
        return pltpu.make_async_remote_copy(
            src_ref=src,
            dst_ref=dst,
            send_sem=ssem.at[number],
            recv_sem=rsem.at[number],
            device_id=device,
            device_id_type=MESH,
        )

    def send(src, dst, device):
        number = used[0]
        used[0] += 1
        copy = remote(src, dst, number, device)
        copy.start()
        started.append(copy)
        return number

    def landed(dst, number):
        remote(dst, dst, number, twin).wait_recv()

    barrier = pltpu.get_barrier_semaphore()
    near = (twin, right, left, across, mate) if BARRIER_NEAR else peers + [mate]
    for device in near:
        pl.semaphore_signal(barrier, inc=1, device_id=device, device_id_type=MESH)
    loads = [
        pltpu.make_async_copy(val_hbm, val, local_sem.at[0]),
        pltpu.make_async_copy(cot_hbm, cot, local_sem.at[1]),
        pltpu.make_async_copy(hid_hbm, hid, local_sem.at[2]),
    ]
    for load in loads:
        load.start()

    wts[me, :state2] = state_ref[...].astype(BF16)
    wts[me, state2:] = step_ref[...].astype(BF16)
    at_u = lax.broadcasted_iota(jnp.int32, (chunk, chunk), 0)
    at_t = lax.broadcasted_iota(jnp.int32, (chunk, chunk), 1)
    ep_t = jnp.broadcast_to(ep_ref[...].astype(F32), (chunk, chunk))
    mask_s[...] = jnp.where((at_u <= at_t) & (ep_t.T == ep_t), 1.0, 0.0)
    eye_r = lax.broadcasted_iota(jnp.int32, (heads, heads), 0)
    eye_c = lax.broadcasted_iota(jnp.int32, (heads, heads), 1)

    def column(row_ref):
        spread_row = jnp.broadcast_to(row_ref[...], (heads, heads))
        return jnp.sum(jnp.where(eye_r == eye_c, spread_row, 0.0), axis=1, keepdims=True)

    decay = -jnp.exp(column(decay_ref))
    bias_col = column(bias_ref)
    place_r = lax.broadcasted_iota(jnp.int32, (heads, WIDTH), 0)
    place_c = lax.broadcasted_iota(jnp.int32, (heads, WIDTH), 1)
    place_d = jnp.where(place_c == place_r, 1.0, 0.0)
    place_b = jnp.where(place_c == place_r + heads, 1.0, 0.0)
    head_own_s[...] = nn(jnp.broadcast_to(decay_ref[...], (8, heads)), place_d, HIGH) + nn(
        jnp.broadcast_to(bias_ref[...], (8, heads)), place_b, HIGH
    )
    feat[...] = jnp.zeros_like(feat)
    logit_s[...] = jnp.zeros_like(logit_s)
    ds[...] = jnp.zeros_like(ds)

    def prepare(pair, carry):
        for k in range(2):
            h = pair * 2 + k
            lanes = pl.ds(pl.multiple_of(h * WIDTH, WIDTH), WIDTH)
            xh = val[:, lanes]
            gh = cot[:, lanes]
            first = nt(xh[:WIDTH], gh)
            gmat[h, 0] = first[:, :WIDTH]
            gmat[h, 1] = first[:, WIDTH:]
            gmat[h, 2] = nt(xh[WIDTH:], gh[WIDTH:])
        return carry

    pl.semaphore_wait(barrier, len(near))

    top = pl.ds(0, half)
    low = pl.ds(half, half)

    def pass_on(index, part, device):
        return send(wts.at[index, part], wts.at[index, part], device)

    def share(index):
        return send(wts.at[index], wts.at[index], twin)

    def columns(index):
        return pl.ds(pl.multiple_of(index * chunk, chunk), chunk)

    def feat_part(index):
        tokens = hid[:, columns(index)]
        feat[...] += nn(tokens, wts[index, :state2, :])
        logit_s[:, :heads] += nt(tokens, wts[index, state2:, :])

    def shared(z, dx, number):
        index = index_of(z, x_at + dx, other_c)
        landed(wts.at[index], number)
        feat_part(index)

    halves = (top, low)
    n_across = [pass_on(me, part, across) for part in halves]
    n_rt = pass_on(me, top, right)
    n_ll = pass_on(me, low, left)
    n_rl = pass_on(me, low, right)
    n_lt = pass_on(me, top, left)
    n_own = share(me)
    loads[0].wait()
    loads[1].wait()
    lax.fori_loop(0, heads // 2, prepare, 0)
    loads[2].wait()
    feat_part(me)
    shared(z_at, 0, n_own)

    def spread(z, n_rt, n_rl, n_ll, n_lt):
        at_l = index_of(z, x_at + 3, core)
        at_r = index_of(z, x_at + 1, core)
        landed(wts.at[at_l, top], n_rt)
        f_r = pass_on(at_l, top, right)
        landed(wts.at[at_r, low], n_ll)
        f_l = pass_on(at_r, low, left)
        landed(wts.at[at_l, low], n_rl)
        t_l = share(at_l)
        landed(wts.at[at_r, top], n_lt)
        t_r = share(at_r)
        return at_l, at_r, f_r, f_l, t_l, t_r

    at_l, at_r, f_r, f_l, t_l, t_r = spread(z_at, n_rt, n_rl, n_ll, n_lt)
    at_z = index_of(other_z, x_at, core)
    landed(wts.at[at_z, top], n_across[0])
    z_f = pass_on(at_z, top, fwd)
    z_b = pass_on(at_z, top, back)
    landed(wts.at[at_z, low], n_across[1])
    z_2 = pass_on(at_z, low, opposite)
    l_f = pass_on(at_z, low, fwd)
    l_b = pass_on(at_z, low, back)
    t_z = share(at_z)
    feat_part(at_l)
    feat_part(at_r)
    at_2 = index_of(z_at, x_at + 2, core)
    landed(wts.at[at_2, top], f_r)
    landed(wts.at[at_2, low], f_l)
    t_2 = share(at_2)
    feat_part(at_z)
    feat_part(at_2)
    shared(z_at, 3, t_l)
    shared(z_at, 1, t_r)
    far_b = index_of(other_z, x_at + behind, core)
    far_f = index_of(other_z, x_at + ahead, core)
    far_2 = index_of(other_z, x_at + 2, core)
    landed(wts.at[far_b, top], z_f)
    relay = pass_on(far_b, top, fwd)
    shared(other_z, 0, t_z)
    shared(z_at, 2, t_2)
    landed(wts.at[far_f, top], z_b)
    landed(wts.at[far_b, low], l_f)
    t_b = share(far_b)
    landed(wts.at[far_f, low], l_b)
    t_f = share(far_f)
    feat_part(far_b)
    feat_part(far_f)
    landed(wts.at[far_2, low], z_2)
    t_2l = pass_on(far_2, low, twin)
    landed(wts.at[far_2, top], relay)
    t_2t = pass_on(far_2, top, twin)
    feat_part(far_2)
    shared(other_z, ahead, t_b)
    shared(other_z, behind, t_f)
    twin_2 = index_of(other_z, x_at + 2, other_c)
    landed(wts.at[twin_2, low], t_2l)
    landed(wts.at[twin_2, top], t_2t)
    feat_part(twin_2)

    n_part_p = send(wts.at[me], part_p, mate)

    logits = logit_s[...].T[:heads] + bias_col
    small = jnp.exp(-jnp.abs(logits))
    log_part = jnp.where(
        small < 0.01, small * (1.0 - small * (0.5 - small * (1.0 / 3.0))), jnp.log(1.0 + small)
    )
    step = jnp.maximum(logits, 0.0) + log_part
    gate = jnp.where(logits >= 0.0, 1.0, small) / (1.0 + small)
    step_safe = jnp.maximum(step, TINY)
    ratio = jnp.where(logits < -20.0, 1.0, gate / step_safe)
    upper = jnp.where(at_u <= at_t, 1.0, 0.0).astype(BF16)
    c2 = exact(nn, split3(decay * step), upper) * LOG2E
    du = jnp.log2(step_safe) - c2
    du_s[...] = jnp.concatenate([du, jnp.zeros((WIDTH - heads, chunk), F32)], axis=0).T
    c2_s[:, 0, :] = c2
    b_proj = feat[:, :WIDTH]
    c_proj = feat[:, WIDTH:]
    masked = jnp.where(mask_s[...] > 0.5, triple(nt, b_proj, c_proj), 0.0)
    scores[0] = masked[:WIDTH, :WIDTH]
    scores[1] = masked[:WIDTH, WIDTH:]
    scores[2] = masked[WIDTH:, WIDTH:]
    ones8 = jnp.ones((8, chunk), BF16)

    def weigh(h, lane, slot):
        row = c2_s[h, 0:1, :]
        first = jnp.broadcast_to(du_s[:WIDTH, lane : lane + 1], (WIDTH, WIDTH))
        second = jnp.broadcast_to(du_s[WIDTH:, lane : lane + 1], (WIDTH, WIDTH))
        args = (
            jnp.minimum(first + row[:, :WIDTH], CAP),
            first + row[:, WIDTH:],
            jnp.minimum(second + row[:, WIDTH:], CAP),
        )
        for k in range(3):
            e = jnp.exp2(args[k])
            p = gmat[h, k] * e
            ds[k] += p
            vbuf[slot, k] = (e * scores[k]).astype(BF16)
            mbuf[slot, k] = (p * scores[k]).astype(BF16)

    def apply(h, slot):
        lanes = pl.ds(pl.multiple_of(h * WIDTH, WIDTH), WIDTH)
        gh = cot[:, lanes]
        v0 = jnp.concatenate([vbuf[slot, 0], vbuf[slot, 1]], axis=1)
        sgr[:WIDTH, lanes] = nn(v0, gh).astype(BF16)
        sgr[WIDTH:, lanes] = nn(vbuf[slot, 2], gh[WIDTH:]).astype(BF16)
        m0 = jnp.concatenate([mbuf[slot, 0], mbuf[slot, 1]], axis=1)
        m1 = jnp.concatenate([mbuf[slot, 1], mbuf[slot, 2]], axis=0)
        mrow[h, :, :WIDTH] = nn(ones8[:, :WIDTH], mbuf[slot, 0])
        mrow[h, :, WIDTH:] = nn(ones8, m1)
        mcol[h, :, :WIDTH] = nt(ones8, m0)
        mcol[h, :, WIDTH:] = nt(ones8[:, :WIDTH], mbuf[slot, 2])

    weigh(0, 0, 0)

    def head_pair(pair, carry):
        h = pair * 2
        weigh(h + 1, 1, 1)
        apply(h, 0)
        weigh(h + 2, 2, 0)
        apply(h + 1, 1)
        du_s[...] = pltpu.roll(du_s[...], WIDTH - 2, 1)
        return carry

    lax.fori_loop(0, heads // 2 - 1, head_pair, 0)
    weigh(heads - 1, 1, 1)
    apply(heads - 2, 0)
    apply(heads - 1, 1)
    out_sgr = pltpu.make_async_copy(sgr, sgr_hbm, local_sem.at[4])
    out_sgr.start()

    lower = jnp.where(at_u >= at_t, 1.0, 0.0).astype(BF16)
    mc = jnp.sum(mcol[...], axis=1) * 0.125
    drate = exact(nn, split3(jnp.sum(mrow[...], axis=1) * 0.125 - mc), lower)
    dlogit = mc * ratio + gate * (decay * drate)
    ddecay = decay * step * drate
    stack = jnp.concatenate(
        [ddecay, dlogit, jnp.zeros((WIDTH - 2 * heads, chunk), F32)], axis=0
    )
    ds_full = jnp.concatenate(
        [
            jnp.concatenate([ds[0], ds[1]], axis=1),
            jnp.concatenate([jnp.zeros((WIDTH, WIDTH), F32), ds[2]], axis=1),
        ],
        axis=0,
    )
    ds_full = jnp.where(mask_s[...] > 0.5, ds_full, 0.0)
    db = triple(nn, ds_full, c_proj)
    dct = triple(nn, b_proj.T, ds_full)
    fgt[:WIDTH] = db.T.astype(BF16)
    fgt[WIDTH:state2] = dct.astype(BF16)
    fgt[state2:] = dlogit.astype(BF16)

    places = [(z, dx) for z in (other_z, z_at) for dx in (2, ahead, behind, 0)]
    twin_places = [(z, dx) for z in (other_z, z_at) for dx in (2, behind, ahead, 0)]
    n_core = {}

    def twin_part(slot):
        z, dx = twin_places[slot]
        index = index_of(z, x_at + dx, other_c)
        dwo[slot] = nn(fgt[...], hid[:, columns(index)]).astype(BF16)
        n_core[slot] = send(dwo.at[slot], from_core.at[slot], twin)

    def own_part(slot):
        z, dx = places[slot]
        index = index_of(z, x_at + dx, core)
        total = nn(fgt[...], hid[:, columns(index)])
        landed(from_core.at[slot], n_core[slot])
        return total + from_core[slot].astype(F32)

    def layer_part(index):
        spot = columns(index)
        w = wts[index]
        lay[:, spot] = (
            nt(fg[...], w[:state2]) + nn(fgl[:, :heads], w[state2:])
        ).astype(BF16)

    def ring_first(base, k):
        twin_part(base)
        twin_part(base + 1)
        acc[base] = own_part(base).astype(BF16)
        straight = send(acc.at[base, top], direct.at[k], opposite)
        hop = send(acc.at[base, low], hop1.at[k], fwd)
        twin_part(base + 2)
        plus = own_part(base + 1)
        acc[base + 1, top] = plus[:half].astype(BF16)
        keep[k] = plus[half:]
        f_t = send(acc.at[base + 1, top], hop2.at[k, 0, top], fwd)
        twin_part(base + 3)
        acc[base + 2] = own_part(base + 2).astype(BF16)
        b_t = send(acc.at[base + 2, top], hop2.at[k, 1, top], back)
        b_l = send(acc.at[base + 2, low], hop2.at[k, 1, low], back)
        zero_sum[k] = own_part(base + 3)
        return straight, hop, f_t, b_t, b_l

    def ring_next(base, k, hop):
        landed(hop1.at[k], hop)
        acc[base + 1, low] = (keep[k] + hop1[k].astype(F32)).astype(BF16)
        return send(acc.at[base + 1, low], hop2.at[k, 0, low], fwd)

    def ring_end(k, part, from_back, from_fwd):
        landed(hop2.at[k, 0, part], from_back)
        landed(hop2.at[k, 1, part], from_fwd)
        return (
            zero_sum[k, part, :]
            + hop2[k, 0, part, :].astype(F32)
            + hop2[k, 1, part, :].astype(F32)
        )

    def ring_top(k, straight, from_back, from_fwd):
        landed(direct.at[k], straight)
        return ring_end(k, top, from_back, from_fwd) + direct[k].astype(F32)

    straight, hop, f_t, b_t, b_l = ring_first(0, 0)
    f_l = ring_next(0, 0, hop)
    straight2, hop, f_t2, b_t2, b_l2 = ring_first(4, 1)
    zsend[top, :] = ring_top(0, straight, f_t, b_t).astype(BF16)
    n_z = [send(zsend.at[top], from_z.at[top], across)]
    zsend[low, :] = ring_end(0, low, f_l, b_l).astype(BF16)
    n_z.append(send(zsend.at[low], from_z.at[low], across))
    f_l2 = ring_next(4, 1, hop)

    sums8 = exact(lambda a, b: nt(b, a), split3(stack), jnp.ones((8, chunk), BF16))
    heads_in[me] = sums8
    n_heads = [send(heads_in.at[me], heads_in.at[me], device) for device in peers]
    fg[:, :WIDTH] = db.astype(BF16)
    fg[:, WIDTH:] = dct.T.astype(BF16)
    wide = jnp.concatenate([dlogit, jnp.zeros((WIDTH - heads, chunk), F32)], axis=0)
    fgl[...] = wide.T.astype(BF16)
    for index in range(seqs):
        layer_part(index)
    out_lay = pltpu.make_async_copy(lay, lay_hbm, local_sem.at[5])
    out_lay.start()

    for k, number in enumerate(n_heads):
        landed(heads_in.at[lax.rem(me + seqs - k - 1, seqs)], number)
    head_grad = jnp.sum(heads_in[...], axis=0)[:1]
    head_own = head_own_s[:1]
    head_sq = jnp.sum(head_own * head_own, axis=1, keepdims=True) / (2 * heads)
    hgrad_sq = jnp.sum(head_grad * head_grad, axis=1, keepdims=True) / (2 * heads)
    head_trust = jnp.sqrt(head_sq) / jnp.sqrt(hgrad_sq + EPS)
    final_send[...] = jnp.broadcast_to(head_own - RATE * head_trust * head_grad, (8, WIDTH))
    n_final = send(final_send, part_s, mate)
    landed(part_p, n_part_p)

    def lanes_sum(value):
        total = jnp.sum(value * value, axis=0, keepdims=True)
        return total[:, :WIDTH] + total[:, WIDTH:]

    state_own = state_ref[...]
    step_own = step_ref[...]
    own_sq = [lanes_sum(state_own), lanes_sum(step_own)]
    mate_p = part_p[...].astype(F32)
    nstate_ref[...] = 0.5 * (state_own + mate_p[:state2])
    nstep_ref[...] = 0.5 * (step_own + mate_p[state2:])

    n_part_g = {}
    for q in range(2):
        spot = halves[q]
        if q:
            total = ring_end(1, low, f_l2, b_l2)
        else:
            total = ring_top(1, straight2, f_t2, b_t2)
        landed(from_z.at[spot], n_z[q])
        total = total + from_z[spot, :].astype(F32)
        grad_s[spot, :] = total
        gsend[spot, :] = total.astype(BF16)
        n_part_g[q] = send(gsend.at[spot], part_g.at[spot], mate)
    grad = grad_s[...]

    sums_in[me] = jnp.concatenate(
        [lanes_sum(grad[:state2]), lanes_sum(grad[state2:])]
        + own_sq
        + [jnp.zeros((4, WIDTH), F32)],
        axis=0,
    )
    n_sums = [send(sums_in.at[me], sums_in.at[me], device) for device in peers]
    n_mate = [
        send(sums_in.at[me], mate_sums.at[me], dict(mate, fsdp=lax.rem(me + k, seqs)))
        for k in range(seqs)
    ]
    grad_state = grad[:state2].T
    for q in range(2):
        landed(part_g.at[halves[q]], n_part_g[q])
    mate_g = part_g[...].astype(F32)
    mate_state = mate_g[:state2].T
    landed(part_s, n_final)
    head_mix = 0.5 * (final_send[:1] + part_s[:1])
    ndecay_ref[...] = head_mix[:, :heads]
    nbias_ref[...] = head_mix[:, heads : 2 * heads]
    for k, number in enumerate(n_sums):
        landed(sums_in.at[lax.rem(me + seqs - k - 1, seqs)], number)
    for k, number in enumerate(n_mate):
        landed(mate_sums.at[lax.rem(me + seqs - k, seqs)], number)
    width = seqs * chunk

    def trusts(ref):
        squares = jnp.sum(jnp.sum(ref[...], axis=0), axis=1, keepdims=True)
        state_trust = jnp.sqrt(squares[2:3] / (width * state2)) / jnp.sqrt(
            squares[0:1] / (width * state2) + EPS
        )
        step_trust = jnp.sqrt(squares[3:4] / (width * heads)) / jnp.sqrt(
            squares[1:2] / (width * heads) + EPS
        )
        return (0.5 * RATE) * state_trust, (0.5 * RATE) * step_trust

    state_trust, step_trust = trusts(sums_in)
    state_mate, step_mate = trusts(mate_sums)
    nstate_ref[...] -= state_trust * grad_state + state_mate * mate_state
    nstep_ref[...] -= step_trust * grad[state2:] + step_mate * mate_g[state2:]

    out_sgr.wait()
    out_lay.wait()
    for copy in started:
        copy.wait_send()


def place_kernel(*refs):
    count = (len(refs) - 1) // 2
    sem = refs[-1]
    copies = [
        pltpu.make_async_copy(refs[k], refs[count + k], sem.at[k]) for k in range(count)
    ]
    for copy in copies:
        copy.start()
    for copy in copies:
        copy.wait()


def on_device(
    hidden_in, scan_in, grad_out, episodes, gossip_step, state_proj, step_proj, decay_log, step_bias
):
    reps = lax.axis_size("rep")
    seqs = lax.axis_size("fsdp")
    bits = reps.bit_length() - 1
    heads = step_proj.shape[1]
    length, inner = scan_in.shape[2:]
    model = hidden_in.shape[3]
    chunk = model // seqs
    state2 = 2 * WIDTH
    rows = state2 + heads
    half = rows // 2
    vmem = pl.BlockSpec(memory_space=pltpu.VMEM)
    anyspace = pl.BlockSpec(memory_space=pl.ANY)
    copies = 132
    shapes = (
        jax.ShapeDtypeStruct((length, model), BF16),
        jax.ShapeDtypeStruct((length, inner), BF16),
        jax.ShapeDtypeStruct((chunk, state2), F32),
        jax.ShapeDtypeStruct((heads, chunk), F32),
        jax.ShapeDtypeStruct((1, heads), F32),
        jax.ShapeDtypeStruct((1, heads), F32),
    )

    def run(bit, *operands):
        outs = pl.pallas_call(
            functools.partial(layer_kernel, (heads, seqs, chunk, rows, bit)),
            out_shape=shapes,
            in_specs=[vmem] * 5 + [anyspace] * 3,
            out_specs=(anyspace, anyspace, vmem, vmem, vmem, vmem),
            scratch_shapes=[
                pltpu.VMEM((length, model), BF16),
                pltpu.VMEM((length, inner), BF16),
                pltpu.VMEM((length, inner), BF16),
                pltpu.VMEM((seqs, rows, chunk), BF16),
                pltpu.VMEM((heads, 3, WIDTH, WIDTH), F32),
                pltpu.VMEM((8, rows, chunk), BF16),
                pltpu.VMEM((8, rows, chunk), BF16),
                pltpu.VMEM((8, rows, chunk), BF16),
                pltpu.VMEM((2, half, chunk), BF16),
                pltpu.VMEM((2, half, chunk), BF16),
                pltpu.VMEM((2, 2, rows, chunk), BF16),
                pltpu.VMEM((rows, chunk), BF16),
                pltpu.VMEM((rows, chunk), BF16),
                pltpu.VMEM((rows, chunk), BF16),
                pltpu.VMEM((8, WIDTH), F32),
                pltpu.VMEM((seqs, 8, WIDTH), F32),
                pltpu.VMEM((rows, chunk), BF16),
                pltpu.VMEM((rows, chunk), BF16),
                pltpu.VMEM((rows, chunk), F32),
                pltpu.VMEM((2, rows, chunk), F32),
                pltpu.VMEM((2, half, chunk), F32),
                pltpu.VMEM((seqs, 8, WIDTH), F32),
                pltpu.VMEM((seqs, 8, WIDTH), F32),
                pltpu.VMEM((8, WIDTH), F32),
                pltpu.VMEM((8, WIDTH), F32),
                pltpu.VMEM((length, model), BF16),
                pltpu.VMEM((length, inner), BF16),
                pltpu.VMEM((length, state2), F32),
                pltpu.VMEM((length, WIDTH), F32),
                pltpu.VMEM((length, length), F32),
                pltpu.VMEM((length, WIDTH), F32),
                pltpu.VMEM((heads, 8, length), F32),
                pltpu.VMEM((3, WIDTH, WIDTH), F32),
                pltpu.VMEM((3, WIDTH, WIDTH), F32),
                pltpu.VMEM((2, 3, WIDTH, WIDTH), BF16),
                pltpu.VMEM((2, 3, WIDTH, WIDTH), BF16),
                pltpu.VMEM((heads, 8, length), F32),
                pltpu.VMEM((heads, 8, length), F32),
                pltpu.VMEM((rows, length), BF16),
                pltpu.VMEM((length, state2), BF16),
                pltpu.VMEM((length, WIDTH), BF16),
                pltpu.SemaphoreType.DMA((6,)),
                pltpu.SemaphoreType.DMA((copies,)),
                pltpu.SemaphoreType.DMA((copies,)),
            ],
            compiler_params=pltpu.CompilerParams(
                collective_id=bit, has_side_effects=True, vmem_limit_bytes=38 * 1024 * 1024
            ),
        )(*operands)
        return tuple(
            pl.pallas_call(
                place_kernel,
                out_shape=shapes,
                in_specs=[anyspace] * len(shapes),
                out_specs=(anyspace,) * len(shapes),
                scratch_shapes=[pltpu.SemaphoreType.DMA((len(shapes),))],
                compiler_params=pltpu.CompilerParams(vmem_limit_bytes=1024 * 1024),
            )(*outs)
        )

    operands = (
        state_proj[0],
        step_proj[0],
        episodes[0],
        decay_log,
        step_bias,
        hidden_in[0, 0],
        scan_in[0, 0],
        grad_out[0, 0],
    )
    outs = lax.switch(
        lax.rem(gossip_step[0], bits), [functools.partial(run, bit) for bit in range(bits)], *operands
    )
    layer_grad, scan_grad, new_state, new_step, new_decay, new_bias = outs
    return (
        layer_grad[None, None],
        scan_grad[None, None],
        new_state[None],
        new_step[None],
        new_decay,
        new_bias,
    )


def solution(mesh):
    in_specs = (
        P("rep", "fsdp", None, None),
        P("rep", "fsdp", None, None),
        P("rep", "fsdp", None, None),
        P("rep", "fsdp", None),
        P(),
        P("rep", "fsdp", None),
        P("rep", None, "fsdp"),
        P("rep", None),
        P("rep", None),
    )
    out_specs = (
        P("rep", "fsdp", None, None),
        P("rep", "fsdp", None, None),
        P("rep", "fsdp", None),
        P("rep", None, "fsdp"),
        P("rep", None),
        P("rep", None),
    )
    return jax.shard_map(
        on_device, mesh=mesh, in_specs=in_specs, out_specs=out_specs, check_vma=False
    )
```

```python
import functools

import jax
import jax.numpy as jnp
from jax import lax
from jax.experimental import pallas as pl
from jax.experimental.pallas import tpu as pltpu
from jax.sharding import PartitionSpec as P

MESH = pl.DeviceIdType.MESH
F32 = jnp.float32
BF16 = jnp.bfloat16
HIGH = lax.Precision.HIGHEST
LOG2E = 1.4426950408889634
TINY = 1e-37
CAP = 60.0
RATE = 0.1
EPS = 1e-6
WIDTH = 128
BARRIER_NEAR = True
EARLY = 10


def nn(a, b, precision=None):
    return lax.dot_general(
        a, b, (((1,), (0,)), ((), ())), precision=precision, preferred_element_type=F32
    )


def nt(a, b, precision=None):
    return lax.dot_general(
        a, b, (((1,), (1,)), ((), ())), precision=precision, preferred_element_type=F32
    )


def split3(value):
    high = value.astype(BF16).astype(F32)
    rest = value - high
    mid = rest.astype(BF16).astype(F32)
    return high, mid, rest - mid


def split2(value):
    high = value.astype(BF16)
    return high, (value - high.astype(F32)).astype(BF16)


def triple(product, a, b):
    ah, al = split2(a)
    bh, bl = split2(b)
    return product(ah, bh) + (product(ah, bl) + product(al, bh))


def exact(product, parts, b):
    high, mid, low = (part.astype(BF16) for part in parts)
    return product(high, b) + (product(mid, b) + product(low, b))


def layer_kernel(
    dims,
    state_ref,
    step_ref,
    ep_ref,
    decay_ref,
    bias_ref,
    hid_hbm,
    val_hbm,
    cot_hbm,
    lay,
    sgr,
    nstate_ref,
    nstep_ref,
    ndecay_ref,
    nbias_ref,
    hid,
    val,
    cot,
    wts,
    gmat,
    dwo,
    acc,
    from_core,
    hop1,
    direct,
    hop2,
    from_z,
    part_p,
    part_g,
    part_s,
    mate_sums,
    zsend,
    gsend,
    grad_s,
    zero_sum,
    keep,
    heads_in,
    sums_in,
    final_send,
    head_own_s,
    feat,
    logit_s,
    mask_s,
    du_s,
    c2_s,
    scores,
    ds,
    vbuf,
    mbuf,
    mrow,
    mcol,
    fgt,
    fg,
    fgl,
    local_sem,
    ssem,
    rsem,
):
    heads, seqs, chunk, rows, bit = dims
    half = rows // 2
    state2 = 2 * WIDTH
    me = lax.axis_index("fsdp")
    rep = lax.axis_index("rep")
    core = lax.rem(me, 2)
    x_at = lax.rem(lax.div(me, 2), 4)
    z_at = lax.div(me, 8)

    def index_of(z, x, c):
        return z * 8 + lax.rem(x, 4) * 2 + c

    other_z = 1 - z_at
    other_c = 1 - core
    right = {"fsdp": index_of(z_at, x_at + 1, core)}
    left = {"fsdp": index_of(z_at, x_at + 3, core)}
    across = {"fsdp": index_of(other_z, x_at, core)}
    twin = {"fsdp": index_of(z_at, x_at, other_c)}
    ahead = 1 + 2 * core
    behind = 3 - 2 * core
    fwd = {"fsdp": index_of(z_at, x_at + ahead, core)}
    back = {"fsdp": index_of(z_at, x_at + behind, core)}
    opposite = {"fsdp": index_of(z_at, x_at + 2, core)}
    peers = [{"fsdp": lax.rem(me + k, seqs)} for k in range(1, seqs)]
    gap = 1 << bit
    mate = {"rep": rep + gap * (1 - 2 * lax.rem(lax.div(rep, gap), 2))}

    used = [0]
    started = []

    def remote(src, dst, number, device):
        return pltpu.make_async_remote_copy(
            src_ref=src,
            dst_ref=dst,
            send_sem=ssem.at[number],
            recv_sem=rsem.at[number],
            device_id=device,
            device_id_type=MESH,
        )

    def send(src, dst, device):
        number = used[0]
        used[0] += 1
        copy = remote(src, dst, number, device)
        copy.start()
        started.append(copy)
        return number

    def landed(dst, number):
        remote(dst, dst, number, twin).wait_recv()

    barrier = pltpu.get_barrier_semaphore()
    near = (twin, right, left, across, mate) if BARRIER_NEAR else peers + [mate]
    for device in near:
        pl.semaphore_signal(barrier, inc=1, device_id=device, device_id_type=MESH)
    loads = [
        pltpu.make_async_copy(val_hbm, val, local_sem.at[0]),
        pltpu.make_async_copy(cot_hbm, cot, local_sem.at[1]),
        pltpu.make_async_copy(hid_hbm, hid, local_sem.at[2]),
    ]
    for load in loads:
        load.start()

    wts[me, :state2] = state_ref[...].astype(BF16)
    wts[me, state2:] = step_ref[...].astype(BF16)
    at_u = lax.broadcasted_iota(jnp.int32, (chunk, chunk), 0)
    at_t = lax.broadcasted_iota(jnp.int32, (chunk, chunk), 1)
    ep_t = jnp.broadcast_to(ep_ref[...].astype(F32), (chunk, chunk))
    mask_s[...] = jnp.where((at_u <= at_t) & (ep_t.T == ep_t), 1.0, 0.0)
    eye_r = lax.broadcasted_iota(jnp.int32, (heads, heads), 0)
    eye_c = lax.broadcasted_iota(jnp.int32, (heads, heads), 1)

    def column(row_ref):
        spread_row = jnp.broadcast_to(row_ref[...], (heads, heads))
        return jnp.sum(jnp.where(eye_r == eye_c, spread_row, 0.0), axis=1, keepdims=True)

    decay = -jnp.exp(column(decay_ref))
    bias_col = column(bias_ref)
    place_r = lax.broadcasted_iota(jnp.int32, (heads, WIDTH), 0)
    place_c = lax.broadcasted_iota(jnp.int32, (heads, WIDTH), 1)
    place_d = jnp.where(place_c == place_r, 1.0, 0.0)
    place_b = jnp.where(place_c == place_r + heads, 1.0, 0.0)
    head_own_s[...] = nn(jnp.broadcast_to(decay_ref[...], (8, heads)), place_d, HIGH) + nn(
        jnp.broadcast_to(bias_ref[...], (8, heads)), place_b, HIGH
    )
    feat[...] = jnp.zeros_like(feat)
    logit_s[...] = jnp.zeros_like(logit_s)
    ds[...] = jnp.zeros_like(ds)

    def prepare(pair, carry):
        for k in range(2):
            h = pair * 2 + k
            lanes = pl.ds(pl.multiple_of(h * WIDTH, WIDTH), WIDTH)
            xh = val[:, lanes]
            gh = cot[:, lanes]
            first = nt(xh[:WIDTH], gh)
            gmat[h, 0] = first[:, :WIDTH]
            gmat[h, 1] = first[:, WIDTH:]
            gmat[h, 2] = nt(xh[WIDTH:], gh[WIDTH:])
        return carry

    pl.semaphore_wait(barrier, len(near))

    top = pl.ds(0, half)
    low = pl.ds(half, half)

    def pass_on(index, part, device):
        return send(wts.at[index, part], wts.at[index, part], device)

    def share(index):
        return send(wts.at[index], wts.at[index], twin)

    def columns(index):
        return pl.ds(pl.multiple_of(index * chunk, chunk), chunk)

    def feat_part(index):
        tokens = hid[:, columns(index)]
        feat[...] += nn(tokens, wts[index, :state2, :])
        logit_s[:, :heads] += nt(tokens, wts[index, state2:, :])

    def shared(z, dx, number):
        index = index_of(z, x_at + dx, other_c)
        landed(wts.at[index], number)
        feat_part(index)

    halves = (top, low)
    n_across = [pass_on(me, part, across) for part in halves]
    n_rt = pass_on(me, top, right)
    n_ll = pass_on(me, low, left)
    n_rl = pass_on(me, low, right)
    n_lt = pass_on(me, top, left)
    n_own = share(me)
    loads[0].wait()
    loads[1].wait()
    lax.fori_loop(0, heads // 2, prepare, 0)
    loads[2].wait()
    feat_part(me)
    shared(z_at, 0, n_own)

    def spread(z, n_rt, n_rl, n_ll, n_lt):
        at_l = index_of(z, x_at + 3, core)
        at_r = index_of(z, x_at + 1, core)
        landed(wts.at[at_l, top], n_rt)
        f_r = pass_on(at_l, top, right)
        landed(wts.at[at_r, low], n_ll)
        f_l = pass_on(at_r, low, left)
        landed(wts.at[at_l, low], n_rl)
        t_l = share(at_l)
        landed(wts.at[at_r, top], n_lt)
        t_r = share(at_r)
        return at_l, at_r, f_r, f_l, t_l, t_r

    at_l, at_r, f_r, f_l, t_l, t_r = spread(z_at, n_rt, n_rl, n_ll, n_lt)
    at_z = index_of(other_z, x_at, core)
    landed(wts.at[at_z, top], n_across[0])
    def scatter(part):
        return [pass_on(at_z, part, device) for device in (opposite, fwd, back)]

    far = [scatter(top)]
    landed(wts.at[at_z, low], n_across[1])
    far.append(scatter(low))
    t_z = share(at_z)
    feat_part(at_l)
    feat_part(at_r)
    at_2 = index_of(z_at, x_at + 2, core)
    landed(wts.at[at_2, top], f_r)
    landed(wts.at[at_2, low], f_l)
    t_2 = share(at_2)
    feat_part(at_z)
    feat_part(at_2)
    shared(z_at, 3, t_l)
    shared(z_at, 1, t_r)
    far_b = index_of(other_z, x_at + behind, core)
    far_f = index_of(other_z, x_at + ahead, core)
    far_2 = index_of(other_z, x_at + 2, core)
    far_own = (far_2, far_b, far_f)
    far_twin = (
        index_of(other_z, x_at + 2, other_c),
        index_of(other_z, x_at + ahead, other_c),
        index_of(other_z, x_at + behind, other_c),
    )
    shared(other_z, 0, t_z)
    shared(z_at, 2, t_2)
    t_far = {}
    for p, part in enumerate(halves):
        for k in (1, 2, 0):
            landed(wts.at[far_own[k], part], far[p][k])
            t_far[p, k] = pass_on(far_own[k], part, twin)
    for k in (1, 2, 0):
        feat_part(far_own[k])
    for k in (1, 2, 0):
        for p, part in enumerate(halves):
            landed(wts.at[far_twin[k], part], t_far[p, k])
        feat_part(far_twin[k])

    n_part_p = send(wts.at[me], part_p, mate)

    logits = logit_s[...].T[:heads] + bias_col
    small = jnp.exp(-jnp.abs(logits))
    log_part = jnp.where(
        small < 0.01, small * (1.0 - small * (0.5 - small * (1.0 / 3.0))), jnp.log(1.0 + small)
    )
    step = jnp.maximum(logits, 0.0) + log_part
    gate = jnp.where(logits >= 0.0, 1.0, small) / (1.0 + small)
    step_safe = jnp.maximum(step, TINY)
    ratio = jnp.where(logits < -20.0, 1.0, gate / step_safe)
    upper = jnp.where(at_u <= at_t, 1.0, 0.0).astype(BF16)
    c2 = exact(nn, split3(decay * step), upper) * LOG2E
    du = jnp.log2(step_safe) - c2
    du_s[...] = jnp.concatenate([du, jnp.zeros((WIDTH - heads, chunk), F32)], axis=0).T
    c2_s[:, 0, :] = c2
    b_proj = feat[:, :WIDTH]
    c_proj = feat[:, WIDTH:]
    masked = jnp.where(mask_s[...] > 0.5, triple(nt, b_proj, c_proj), 0.0)
    scores[0] = masked[:WIDTH, :WIDTH]
    scores[1] = masked[:WIDTH, WIDTH:]
    scores[2] = masked[WIDTH:, WIDTH:]
    ones8 = jnp.ones((8, chunk), BF16)

    def weigh(h, lane, slot):
        row = c2_s[h, 0:1, :]
        first = jnp.broadcast_to(du_s[:WIDTH, lane : lane + 1], (WIDTH, WIDTH))
        second = jnp.broadcast_to(du_s[WIDTH:, lane : lane + 1], (WIDTH, WIDTH))
        args = (
            jnp.minimum(first + row[:, :WIDTH], CAP),
            first + row[:, WIDTH:],
            jnp.minimum(second + row[:, WIDTH:], CAP),
        )
        for k in range(3):
            e = jnp.exp2(args[k])
            p = gmat[h, k] * e
            ds[k] += p
            vbuf[slot, k] = (e * scores[k]).astype(BF16)
            mbuf[slot, k] = (p * scores[k]).astype(BF16)

    def apply(h, slot):
        lanes = pl.ds(pl.multiple_of(h * WIDTH, WIDTH), WIDTH)
        gh = cot[:, lanes]
        v0 = jnp.concatenate([vbuf[slot, 0], vbuf[slot, 1]], axis=1)
        sgr[:WIDTH, lanes] = nn(v0, gh).astype(BF16)
        sgr[WIDTH:, lanes] = nn(vbuf[slot, 2], gh[WIDTH:]).astype(BF16)
        m0 = jnp.concatenate([mbuf[slot, 0], mbuf[slot, 1]], axis=1)
        m1 = jnp.concatenate([mbuf[slot, 1], mbuf[slot, 2]], axis=0)
        mrow[h, :, :WIDTH] = nn(ones8[:, :WIDTH], mbuf[slot, 0])
        mrow[h, :, WIDTH:] = nn(ones8, m1)
        mcol[h, :, :WIDTH] = nt(ones8, m0)
        mcol[h, :, WIDTH:] = nt(ones8[:, :WIDTH], mbuf[slot, 2])

    weigh(0, 0, 0)

    def head_pair(pair, carry):
        h = pair * 2
        weigh(h + 1, 1, 1)
        apply(h, 0)
        weigh(h + 2, 2, 0)
        apply(h + 1, 1)
        du_s[...] = pltpu.roll(du_s[...], WIDTH - 2, 1)
        return carry

    lax.fori_loop(0, heads // 2 - 1, head_pair, 0)
    weigh(heads - 1, 1, 1)
    apply(heads - 2, 0)
    apply(heads - 1, 1)

    lower = jnp.where(at_u >= at_t, 1.0, 0.0).astype(BF16)
    mc = jnp.sum(mcol[...], axis=1) * 0.125
    drate = exact(nn, split3(jnp.sum(mrow[...], axis=1) * 0.125 - mc), lower)
    dlogit = mc * ratio + gate * (decay * drate)
    ddecay = decay * step * drate
    stack = jnp.concatenate(
        [ddecay, dlogit, jnp.zeros((WIDTH - 2 * heads, chunk), F32)], axis=0
    )
    ds_full = jnp.concatenate(
        [
            jnp.concatenate([ds[0], ds[1]], axis=1),
            jnp.concatenate([jnp.zeros((WIDTH, WIDTH), F32), ds[2]], axis=1),
        ],
        axis=0,
    )
    ds_full = jnp.where(mask_s[...] > 0.5, ds_full, 0.0)
    db = triple(nn, ds_full, c_proj)
    dct = triple(nn, b_proj.T, ds_full)
    fgt[:WIDTH] = db.T.astype(BF16)
    fgt[WIDTH:state2] = dct.astype(BF16)
    fgt[state2:] = dlogit.astype(BF16)

    places = [(z, dx) for z in (other_z, z_at) for dx in (2, ahead, behind, 0)]
    twin_places = [(z, dx) for z in (other_z, z_at) for dx in (2, behind, ahead, 0)]
    n_core = {}

    def twin_part(slot):
        z, dx = twin_places[slot]
        index = index_of(z, x_at + dx, other_c)
        dwo[slot] = nn(fgt[...], hid[:, columns(index)]).astype(BF16)
        n_core[slot] = send(dwo.at[slot], from_core.at[slot], twin)

    def own_part(slot):
        z, dx = places[slot]
        index = index_of(z, x_at + dx, core)
        total = nn(fgt[...], hid[:, columns(index)])
        landed(from_core.at[slot], n_core[slot])
        return total + from_core[slot].astype(F32)

    def layer_part(index):
        spot = columns(index)
        w = wts[index]
        lay[:, spot] = (
            nt(fg[...], w[:state2]) + nn(fgl[:, :heads], w[state2:])
        ).astype(BF16)

    def ring_first(base, k):
        twin_part(base)
        twin_part(base + 1)
        acc[base] = own_part(base).astype(BF16)
        straight = send(acc.at[base, top], direct.at[k, top], opposite)
        hop = send(acc.at[base, low], hop1.at[k], fwd)
        twin_part(base + 2)
        plus = own_part(base + 1)
        acc[base + 1, top] = plus[:half].astype(BF16)
        keep[k] = plus[half:]
        f_t = send(acc.at[base + 1, top], hop2.at[k, 0, top], fwd)
        twin_part(base + 3)
        acc[base + 2] = own_part(base + 2).astype(BF16)
        b_t = send(acc.at[base + 2, top], hop2.at[k, 1, top], back)
        b_l = send(acc.at[base + 2, low], hop2.at[k, 1, low], back)
        zero_sum[k] = own_part(base + 3)
        return straight, hop, f_t, b_t, b_l

    def ring_next(base, k, hop):
        landed(hop1.at[k], hop)
        acc[base + 1, low] = (keep[k] + hop1[k].astype(F32)).astype(BF16)
        return send(acc.at[base + 1, low], hop2.at[k, 0, low], fwd)

    def ring_end(k, part, from_back, from_fwd):
        landed(hop2.at[k, 0, part], from_back)
        landed(hop2.at[k, 1, part], from_fwd)
        return (
            zero_sum[k, part, :]
            + hop2[k, 0, part, :].astype(F32)
            + hop2[k, 1, part, :].astype(F32)
        )

    def ring_top(k, straight, from_back, from_fwd):
        landed(direct.at[k, top], straight)
        return ring_end(k, top, from_back, from_fwd) + direct[k, top, :].astype(F32)

    twin_part(0)
    twin_part(1)
    acc[0] = own_part(0).astype(BF16)
    ways = ((0, direct.at[0], opposite), (1, hop2.at[0, 0], fwd), (2, hop2.at[0, 1], back))
    far = {}

    def straight_send(k, p):
        slot, into, device = ways[k]
        far[k, p] = send(acc.at[slot, halves[p]], into.at[halves[p]], device)

    straight_send(0, 0)
    twin_part(2)
    acc[1] = own_part(1).astype(BF16)
    straight_send(1, 0)
    twin_part(3)
    acc[2] = own_part(2).astype(BF16)
    straight_send(2, 0)
    for k in range(3):
        straight_send(k, 1)
    zero_sum[0] = own_part(3)
    straight2, hop, f_t2, b_t2, b_l2 = ring_first(4, 1)
    fg[:, :WIDTH] = db.astype(BF16)
    fg[:, WIDTH:] = dct.T.astype(BF16)
    wide = jnp.concatenate([dlogit, jnp.zeros((WIDTH - heads, chunk), F32)], axis=0)
    fgl[...] = wide.T.astype(BF16)
    for index in range(EARLY):
        layer_part(index)
    n_z = []
    for p, part in enumerate(halves):
        for k in range(3):
            landed(ways[k][1].at[part], far[k, p])
        zsend[part, :] = (
            zero_sum[0, part, :]
            + direct[0, part, :].astype(F32)
            + hop2[0, 0, part, :].astype(F32)
            + hop2[0, 1, part, :].astype(F32)
        ).astype(BF16)
        n_z.append(send(zsend.at[part], from_z.at[part], across))
    f_l2 = ring_next(4, 1, hop)

    sums8 = exact(lambda a, b: nt(b, a), split3(stack), jnp.ones((8, chunk), BF16))
    heads_in[me] = sums8
    n_heads = [send(heads_in.at[me], heads_in.at[me], device) for device in peers]
    for index in range(EARLY, seqs):
        layer_part(index)

    for k, number in enumerate(n_heads):
        landed(heads_in.at[lax.rem(me + seqs - k - 1, seqs)], number)
    head_grad = jnp.sum(heads_in[...], axis=0)[:1]
    head_own = head_own_s[:1]
    head_sq = jnp.sum(head_own * head_own, axis=1, keepdims=True) / (2 * heads)
    hgrad_sq = jnp.sum(head_grad * head_grad, axis=1, keepdims=True) / (2 * heads)
    head_trust = jnp.sqrt(head_sq) / jnp.sqrt(hgrad_sq + EPS)
    final_send[...] = jnp.broadcast_to(head_own - RATE * head_trust * head_grad, (8, WIDTH))
    n_final = send(final_send, part_s, mate)
    landed(part_p, n_part_p)

    def lanes_sum(value):
        total = jnp.sum(value * value, axis=0, keepdims=True)
        return total[:, :WIDTH] + total[:, WIDTH:]

    state_own = state_ref[...]
    step_own = step_ref[...]
    own_sq = [lanes_sum(state_own), lanes_sum(step_own)]
    mate_p = part_p[...].astype(F32)
    nstate_ref[...] = 0.5 * (state_own + mate_p[:state2])
    nstep_ref[...] = 0.5 * (step_own + mate_p[state2:])

    n_part_g = {}
    for q in range(2):
        spot = halves[q]
        if q:
            total = ring_end(1, low, f_l2, b_l2)
        else:
            total = ring_top(1, straight2, f_t2, b_t2)
        landed(from_z.at[spot], n_z[q])
        total = total + from_z[spot, :].astype(F32)
        grad_s[spot, :] = total
        gsend[spot, :] = total.astype(BF16)
        n_part_g[q] = send(gsend.at[spot], part_g.at[spot], mate)
    grad = grad_s[...]

    sums_in[me] = jnp.concatenate(
        [lanes_sum(grad[:state2]), lanes_sum(grad[state2:])]
        + own_sq
        + [jnp.zeros((4, WIDTH), F32)],
        axis=0,
    )
    n_sums = [send(sums_in.at[me], sums_in.at[me], device) for device in peers]
    n_mate = [
        send(sums_in.at[me], mate_sums.at[me], dict(mate, fsdp=lax.rem(me + k, seqs)))
        for k in range(seqs)
    ]
    grad_state = grad[:state2].T
    for q in range(2):
        landed(part_g.at[halves[q]], n_part_g[q])
    mate_g = part_g[...].astype(F32)
    mate_state = mate_g[:state2].T
    landed(part_s, n_final)
    head_mix = 0.5 * (final_send[:1] + part_s[:1])
    ndecay_ref[...] = head_mix[:, :heads]
    nbias_ref[...] = head_mix[:, heads : 2 * heads]
    for k, number in enumerate(n_sums):
        landed(sums_in.at[lax.rem(me + seqs - k - 1, seqs)], number)
    for k, number in enumerate(n_mate):
        landed(mate_sums.at[lax.rem(me + seqs - k, seqs)], number)
    width = seqs * chunk

    def trusts(ref):
        squares = jnp.sum(jnp.sum(ref[...], axis=0), axis=1, keepdims=True)
        state_trust = jnp.sqrt(squares[2:3] / (width * state2)) / jnp.sqrt(
            squares[0:1] / (width * state2) + EPS
        )
        step_trust = jnp.sqrt(squares[3:4] / (width * heads)) / jnp.sqrt(
            squares[1:2] / (width * heads) + EPS
        )
        return (0.5 * RATE) * state_trust, (0.5 * RATE) * step_trust

    state_trust, step_trust = trusts(sums_in)
    state_mate, step_mate = trusts(mate_sums)
    nstate_ref[...] -= state_trust * grad_state + state_mate * mate_state
    nstep_ref[...] -= step_trust * grad[state2:] + step_mate * mate_g[state2:]

    for copy in started:
        copy.wait_send()


def place_kernel(*refs):
    count = (len(refs) - 1) // 2
    sem = refs[-1]
    copies = [
        pltpu.make_async_copy(refs[k], refs[count + k], sem.at[k]) for k in range(count)
    ]
    for copy in copies:
        copy.start()
    for copy in copies:
        copy.wait()


def on_device(
    hidden_in, scan_in, grad_out, episodes, gossip_step, state_proj, step_proj, decay_log, step_bias
):
    reps = lax.axis_size("rep")
    seqs = lax.axis_size("fsdp")
    bits = reps.bit_length() - 1
    heads = step_proj.shape[1]
    length, inner = scan_in.shape[2:]
    model = hidden_in.shape[3]
    chunk = model // seqs
    state2 = 2 * WIDTH
    rows = state2 + heads
    half = rows // 2
    vmem = pl.BlockSpec(memory_space=pltpu.VMEM)
    anyspace = pl.BlockSpec(memory_space=pl.ANY)
    copies = 132
    shapes = (
        jax.ShapeDtypeStruct((length, model), BF16),
        jax.ShapeDtypeStruct((length, inner), BF16),
        jax.ShapeDtypeStruct((chunk, state2), F32),
        jax.ShapeDtypeStruct((heads, chunk), F32),
        jax.ShapeDtypeStruct((1, heads), F32),
        jax.ShapeDtypeStruct((1, heads), F32),
    )

    def run(bit, *operands):
        outs = pl.pallas_call(
            functools.partial(layer_kernel, (heads, seqs, chunk, rows, bit)),
            out_shape=shapes,
            in_specs=[vmem] * 5 + [anyspace] * 3,
            out_specs=(vmem,) * len(shapes),
            scratch_shapes=[
                pltpu.VMEM((length, model), BF16),
                pltpu.VMEM((length, inner), BF16),
                pltpu.VMEM((length, inner), BF16),
                pltpu.VMEM((seqs, rows, chunk), BF16),
                pltpu.VMEM((heads, 3, WIDTH, WIDTH), F32),
                pltpu.VMEM((8, rows, chunk), BF16),
                pltpu.VMEM((8, rows, chunk), BF16),
                pltpu.VMEM((8, rows, chunk), BF16),
                pltpu.VMEM((2, half, chunk), BF16),
                pltpu.VMEM((2, rows, chunk), BF16),
                pltpu.VMEM((2, 2, rows, chunk), BF16),
                pltpu.VMEM((rows, chunk), BF16),
                pltpu.VMEM((rows, chunk), BF16),
                pltpu.VMEM((rows, chunk), BF16),
                pltpu.VMEM((8, WIDTH), F32),
                pltpu.VMEM((seqs, 8, WIDTH), F32),
                pltpu.VMEM((rows, chunk), BF16),
                pltpu.VMEM((rows, chunk), BF16),
                pltpu.VMEM((rows, chunk), F32),
                pltpu.VMEM((2, rows, chunk), F32),
                pltpu.VMEM((2, half, chunk), F32),
                pltpu.VMEM((seqs, 8, WIDTH), F32),
                pltpu.VMEM((seqs, 8, WIDTH), F32),
                pltpu.VMEM((8, WIDTH), F32),
                pltpu.VMEM((8, WIDTH), F32),
                pltpu.VMEM((length, state2), F32),
                pltpu.VMEM((length, WIDTH), F32),
                pltpu.VMEM((length, length), F32),
                pltpu.VMEM((length, WIDTH), F32),
                pltpu.VMEM((heads, 8, length), F32),
                pltpu.VMEM((3, WIDTH, WIDTH), F32),
                pltpu.VMEM((3, WIDTH, WIDTH), F32),
                pltpu.VMEM((2, 3, WIDTH, WIDTH), BF16),
                pltpu.VMEM((2, 3, WIDTH, WIDTH), BF16),
                pltpu.VMEM((heads, 8, length), F32),
                pltpu.VMEM((heads, 8, length), F32),
                pltpu.VMEM((rows, length), BF16),
                pltpu.VMEM((length, state2), BF16),
                pltpu.VMEM((length, WIDTH), BF16),
                pltpu.SemaphoreType.DMA((3,)),
                pltpu.SemaphoreType.DMA((copies,)),
                pltpu.SemaphoreType.DMA((copies,)),
            ],
            compiler_params=pltpu.CompilerParams(
                collective_id=bit, has_side_effects=True, vmem_limit_bytes=38 * 1024 * 1024
            ),
        )(*operands)
        return tuple(
            pl.pallas_call(
                place_kernel,
                out_shape=shapes,
                in_specs=[anyspace] * len(shapes),
                out_specs=(anyspace,) * len(shapes),
                scratch_shapes=[pltpu.SemaphoreType.DMA((len(shapes),))],
                compiler_params=pltpu.CompilerParams(vmem_limit_bytes=1024 * 1024),
            )(*outs)
        )

    operands = (
        state_proj[0],
        step_proj[0],
        episodes[0],
        decay_log,
        step_bias,
        hidden_in[0, 0],
        scan_in[0, 0],
        grad_out[0, 0],
    )
    outs = lax.switch(
        lax.rem(gossip_step[0], bits), [functools.partial(run, bit) for bit in range(bits)], *operands
    )
    layer_grad, scan_grad, new_state, new_step, new_decay, new_bias = outs
    return (
        layer_grad[None, None],
        scan_grad[None, None],
        new_state[None],
        new_step[None],
        new_decay,
        new_bias,
    )


def solution(mesh):
    in_specs = (
        P("rep", "fsdp", None, None),
        P("rep", "fsdp", None, None),
        P("rep", "fsdp", None, None),
        P("rep", "fsdp", None),
        P(),
        P("rep", "fsdp", None),
        P("rep", None, "fsdp"),
        P("rep", None),
        P("rep", None),
    )
    out_specs = (
        P("rep", "fsdp", None, None),
        P("rep", "fsdp", None, None),
        P("rep", "fsdp", None),
        P("rep", None, "fsdp"),
        P("rep", None),
        P("rep", None),
    )
    return jax.shard_map(
        on_device, mesh=mesh, in_specs=in_specs, out_specs=out_specs, check_vma=False
    )
```

```python
import functools

import jax
import jax.numpy as jnp
from jax import lax
from jax.experimental import pallas as pl
from jax.experimental.pallas import tpu as pltpu
from jax.sharding import PartitionSpec as P

MESH = pl.DeviceIdType.MESH
F32 = jnp.float32
BF16 = jnp.bfloat16
HIGH = lax.Precision.HIGHEST
LOG2E = 1.4426950408889634
TINY = 1e-37
CAP = 60.0
RATE = 0.1
EPS = 1e-6
WIDTH = 128
BARRIER_NEAR = True
EARLY = 10


def nn(a, b, precision=None):
    return lax.dot_general(
        a, b, (((1,), (0,)), ((), ())), precision=precision, preferred_element_type=F32
    )


def nt(a, b, precision=None):
    return lax.dot_general(
        a, b, (((1,), (1,)), ((), ())), precision=precision, preferred_element_type=F32
    )


def split3(value):
    high = value.astype(BF16).astype(F32)
    rest = value - high
    mid = rest.astype(BF16).astype(F32)
    return high, mid, rest - mid


def split2(value):
    high = value.astype(BF16)
    return high, (value - high.astype(F32)).astype(BF16)


def triple(product, a, b):
    ah, al = split2(a)
    bh, bl = split2(b)
    return product(ah, bh) + (product(ah, bl) + product(al, bh))


def exact(product, parts, b):
    high, mid, low = (part.astype(BF16) for part in parts)
    return product(high, b) + (product(mid, b) + product(low, b))


def layer_kernel(
    dims,
    state_hbm,
    step_hbm,
    ep_hbm,
    decay_hbm,
    bias_hbm,
    hid_hbm,
    val_hbm,
    cot_hbm,
    lay,
    sgr,
    nstate_ref,
    nstep_ref,
    ndecay_ref,
    nbias_ref,
    state_ref,
    step_ref,
    ep_ref,
    decay_ref,
    bias_ref,
    hid,
    val,
    cot,
    wts,
    gmat,
    dwo,
    acc,
    from_core,
    hop1,
    direct,
    hop2,
    from_z,
    part_p,
    part_g,
    part_s,
    mate_sums,
    zsend,
    gsend,
    grad_s,
    zero_sum,
    keep,
    heads_in,
    sums_in,
    final_send,
    head_own_s,
    feat,
    logit_s,
    mask_s,
    du_s,
    c2_s,
    scores,
    ds,
    vbuf,
    mbuf,
    mrow,
    mcol,
    fgt,
    fg,
    fgl,
    local_sem,
    ssem,
    rsem,
):
    heads, seqs, chunk, rows, bit = dims
    half = rows // 2
    state2 = 2 * WIDTH
    me = lax.axis_index("fsdp")
    rep = lax.axis_index("rep")
    core = lax.rem(me, 2)
    x_at = lax.rem(lax.div(me, 2), 4)
    z_at = lax.div(me, 8)

    def index_of(z, x, c):
        return z * 8 + lax.rem(x, 4) * 2 + c

    other_z = 1 - z_at
    other_c = 1 - core
    right = {"fsdp": index_of(z_at, x_at + 1, core)}
    left = {"fsdp": index_of(z_at, x_at + 3, core)}
    across = {"fsdp": index_of(other_z, x_at, core)}
    twin = {"fsdp": index_of(z_at, x_at, other_c)}
    ahead = 1 + 2 * core
    behind = 3 - 2 * core
    fwd = {"fsdp": index_of(z_at, x_at + ahead, core)}
    back = {"fsdp": index_of(z_at, x_at + behind, core)}
    opposite = {"fsdp": index_of(z_at, x_at + 2, core)}
    peers = [{"fsdp": lax.rem(me + k, seqs)} for k in range(1, seqs)]
    gap = 1 << bit
    mate = {"rep": rep + gap * (1 - 2 * lax.rem(lax.div(rep, gap), 2))}

    used = [0]
    started = []

    def remote(src, dst, number, device):
        return pltpu.make_async_remote_copy(
            src_ref=src,
            dst_ref=dst,
            send_sem=ssem.at[number],
            recv_sem=rsem.at[number],
            device_id=device,
            device_id_type=MESH,
        )

    def send(src, dst, device):
        number = used[0]
        used[0] += 1
        copy = remote(src, dst, number, device)
        copy.start()
        started.append(copy)
        return number

    def landed(dst, number):
        remote(dst, dst, number, twin).wait_recv()

    barrier = pltpu.get_barrier_semaphore()
    near = (twin, right, left, across, mate) if BARRIER_NEAR else peers + [mate]
    for device in near:
        pl.semaphore_signal(barrier, inc=1, device_id=device, device_id_type=MESH)
    small_loads = [
        pltpu.make_async_copy(src, dst, local_sem.at[3 + k])
        for k, (src, dst) in enumerate(
            (
                (state_hbm, state_ref),
                (step_hbm, step_ref),
                (ep_hbm, ep_ref),
                (decay_hbm, decay_ref),
                (bias_hbm, bias_ref),
            )
        )
    ]
    for load in small_loads:
        load.start()
    loads = [
        pltpu.make_async_copy(val_hbm, val, local_sem.at[0]),
        pltpu.make_async_copy(cot_hbm, cot, local_sem.at[1]),
        pltpu.make_async_copy(hid_hbm, hid, local_sem.at[2]),
    ]
    for load in loads:
        load.start()

    for load in small_loads:
        load.wait()
    wts[me, :state2] = state_ref[...].astype(BF16)
    wts[me, state2:] = step_ref[...].astype(BF16)
    at_u = lax.broadcasted_iota(jnp.int32, (chunk, chunk), 0)
    at_t = lax.broadcasted_iota(jnp.int32, (chunk, chunk), 1)
    ep_t = jnp.broadcast_to(ep_ref[...].astype(F32), (chunk, chunk))
    mask_s[...] = jnp.where((at_u <= at_t) & (ep_t.T == ep_t), 1.0, 0.0)
    eye_r = lax.broadcasted_iota(jnp.int32, (heads, heads), 0)
    eye_c = lax.broadcasted_iota(jnp.int32, (heads, heads), 1)

    def column(row_ref):
        spread_row = jnp.broadcast_to(row_ref[...], (heads, heads))
        return jnp.sum(jnp.where(eye_r == eye_c, spread_row, 0.0), axis=1, keepdims=True)

    decay = -jnp.exp(column(decay_ref))
    bias_col = column(bias_ref)
    place_r = lax.broadcasted_iota(jnp.int32, (heads, WIDTH), 0)
    place_c = lax.broadcasted_iota(jnp.int32, (heads, WIDTH), 1)
    place_d = jnp.where(place_c == place_r, 1.0, 0.0)
    place_b = jnp.where(place_c == place_r + heads, 1.0, 0.0)
    head_own_s[...] = nn(jnp.broadcast_to(decay_ref[...], (8, heads)), place_d, HIGH) + nn(
        jnp.broadcast_to(bias_ref[...], (8, heads)), place_b, HIGH
    )
    feat[...] = jnp.zeros_like(feat)
    logit_s[...] = jnp.zeros_like(logit_s)
    ds[...] = jnp.zeros_like(ds)

    def prepare(pair, carry):
        for k in range(2):
            h = pair * 2 + k
            lanes = pl.ds(pl.multiple_of(h * WIDTH, WIDTH), WIDTH)
            xh = val[:, lanes]
            gh = cot[:, lanes]
            first = nt(xh[:WIDTH], gh)
            gmat[h, 0] = first[:, :WIDTH]
            gmat[h, 1] = first[:, WIDTH:]
            gmat[h, 2] = nt(xh[WIDTH:], gh[WIDTH:])
        return carry

    pl.semaphore_wait(barrier, len(near))

    top = pl.ds(0, half)
    low = pl.ds(half, half)

    def pass_on(index, part, device):
        return send(wts.at[index, part], wts.at[index, part], device)

    def share(index):
        return send(wts.at[index], wts.at[index], twin)

    def columns(index):
        return pl.ds(pl.multiple_of(index * chunk, chunk), chunk)

    def feat_part(index):
        tokens = hid[:, columns(index)]
        feat[...] += nn(tokens, wts[index, :state2, :])
        logit_s[:, :heads] += nt(tokens, wts[index, state2:, :])

    def shared(z, dx, number):
        index = index_of(z, x_at + dx, other_c)
        landed(wts.at[index], number)
        feat_part(index)

    halves = (top, low)
    n_across = [pass_on(me, part, across) for part in halves]
    n_rt = pass_on(me, top, right)
    n_ll = pass_on(me, low, left)
    n_rl = pass_on(me, low, right)
    n_lt = pass_on(me, top, left)
    n_own = share(me)
    loads[0].wait()
    loads[1].wait()
    lax.fori_loop(0, heads // 2, prepare, 0)
    loads[2].wait()
    feat_part(me)
    shared(z_at, 0, n_own)

    def spread(z, n_rt, n_rl, n_ll, n_lt):
        at_l = index_of(z, x_at + 3, core)
        at_r = index_of(z, x_at + 1, core)
        landed(wts.at[at_l, top], n_rt)
        f_r = pass_on(at_l, top, right)
        landed(wts.at[at_r, low], n_ll)
        f_l = pass_on(at_r, low, left)
        landed(wts.at[at_l, low], n_rl)
        t_l = share(at_l)
        landed(wts.at[at_r, top], n_lt)
        t_r = share(at_r)
        return at_l, at_r, f_r, f_l, t_l, t_r

    at_l, at_r, f_r, f_l, t_l, t_r = spread(z_at, n_rt, n_rl, n_ll, n_lt)
    at_z = index_of(other_z, x_at, core)
    landed(wts.at[at_z, top], n_across[0])
    def scatter(part):
        return [pass_on(at_z, part, device) for device in (opposite, fwd, back)]

    far = [scatter(top)]
    landed(wts.at[at_z, low], n_across[1])
    far.append(scatter(low))
    t_z = share(at_z)
    feat_part(at_l)
    feat_part(at_r)
    at_2 = index_of(z_at, x_at + 2, core)
    landed(wts.at[at_2, top], f_r)
    landed(wts.at[at_2, low], f_l)
    t_2 = share(at_2)
    feat_part(at_z)
    feat_part(at_2)
    shared(z_at, 3, t_l)
    shared(z_at, 1, t_r)
    far_b = index_of(other_z, x_at + behind, core)
    far_f = index_of(other_z, x_at + ahead, core)
    far_2 = index_of(other_z, x_at + 2, core)
    far_own = (far_2, far_b, far_f)
    far_twin = (
        index_of(other_z, x_at + 2, other_c),
        index_of(other_z, x_at + ahead, other_c),
        index_of(other_z, x_at + behind, other_c),
    )
    shared(other_z, 0, t_z)
    shared(z_at, 2, t_2)
    t_far = {}
    for p, part in enumerate(halves):
        for k in (1, 2, 0):
            landed(wts.at[far_own[k], part], far[p][k])
            t_far[p, k] = pass_on(far_own[k], part, twin)
    for k in (1, 2, 0):
        feat_part(far_own[k])
    for k in (1, 2, 0):
        for p, part in enumerate(halves):
            landed(wts.at[far_twin[k], part], t_far[p, k])
        feat_part(far_twin[k])

    n_part_p = send(wts.at[me], part_p, mate)

    logits = logit_s[...].T[:heads] + bias_col
    small = jnp.exp(-jnp.abs(logits))
    log_part = jnp.where(
        small < 0.01, small * (1.0 - small * (0.5 - small * (1.0 / 3.0))), jnp.log(1.0 + small)
    )
    step = jnp.maximum(logits, 0.0) + log_part
    gate = jnp.where(logits >= 0.0, 1.0, small) / (1.0 + small)
    step_safe = jnp.maximum(step, TINY)
    ratio = jnp.where(logits < -20.0, 1.0, gate / step_safe)
    upper = jnp.where(at_u <= at_t, 1.0, 0.0).astype(BF16)
    c2 = exact(nn, split3(decay * step), upper) * LOG2E
    du = jnp.log2(step_safe) - c2
    du_s[...] = jnp.concatenate([du, jnp.zeros((WIDTH - heads, chunk), F32)], axis=0).T
    c2_s[:, 0, :] = c2
    b_proj = feat[:, :WIDTH]
    c_proj = feat[:, WIDTH:]
    masked = jnp.where(mask_s[...] > 0.5, triple(nt, b_proj, c_proj), 0.0)
    scores[0] = masked[:WIDTH, :WIDTH]
    scores[1] = masked[:WIDTH, WIDTH:]
    scores[2] = masked[WIDTH:, WIDTH:]
    ones8 = jnp.ones((8, chunk), BF16)

    def weigh(h, lane, slot):
        row = c2_s[h, 0:1, :]
        first = jnp.broadcast_to(du_s[:WIDTH, lane : lane + 1], (WIDTH, WIDTH))
        second = jnp.broadcast_to(du_s[WIDTH:, lane : lane + 1], (WIDTH, WIDTH))
        args = (
            jnp.minimum(first + row[:, :WIDTH], CAP),
            first + row[:, WIDTH:],
            jnp.minimum(second + row[:, WIDTH:], CAP),
        )
        for k in range(3):
            e = jnp.exp2(args[k])
            p = gmat[h, k] * e
            ds[k] += p
            vbuf[slot, k] = (e * scores[k]).astype(BF16)
            mbuf[slot, k] = (p * scores[k]).astype(BF16)

    def apply(h, slot):
        lanes = pl.ds(pl.multiple_of(h * WIDTH, WIDTH), WIDTH)
        gh = cot[:, lanes]
        v0 = jnp.concatenate([vbuf[slot, 0], vbuf[slot, 1]], axis=1)
        sgr[:WIDTH, lanes] = nn(v0, gh).astype(BF16)
        sgr[WIDTH:, lanes] = nn(vbuf[slot, 2], gh[WIDTH:]).astype(BF16)
        m0 = jnp.concatenate([mbuf[slot, 0], mbuf[slot, 1]], axis=1)
        m1 = jnp.concatenate([mbuf[slot, 1], mbuf[slot, 2]], axis=0)
        mrow[h, :, :WIDTH] = nn(ones8[:, :WIDTH], mbuf[slot, 0])
        mrow[h, :, WIDTH:] = nn(ones8, m1)
        mcol[h, :, :WIDTH] = nt(ones8, m0)
        mcol[h, :, WIDTH:] = nt(ones8[:, :WIDTH], mbuf[slot, 2])

    weigh(0, 0, 0)

    def head_pair(pair, carry):
        h = pair * 2
        weigh(h + 1, 1, 1)
        apply(h, 0)
        weigh(h + 2, 2, 0)
        apply(h + 1, 1)
        du_s[...] = pltpu.roll(du_s[...], WIDTH - 2, 1)
        return carry

    lax.fori_loop(0, heads // 2 - 1, head_pair, 0)
    weigh(heads - 1, 1, 1)
    apply(heads - 2, 0)
    apply(heads - 1, 1)

    lower = jnp.where(at_u >= at_t, 1.0, 0.0).astype(BF16)
    mc = jnp.sum(mcol[...], axis=1) * 0.125
    drate = exact(nn, split3(jnp.sum(mrow[...], axis=1) * 0.125 - mc), lower)
    dlogit = mc * ratio + gate * (decay * drate)
    ddecay = decay * step * drate
    stack = jnp.concatenate(
        [ddecay, dlogit, jnp.zeros((WIDTH - 2 * heads, chunk), F32)], axis=0
    )
    ds_full = jnp.concatenate(
        [
            jnp.concatenate([ds[0], ds[1]], axis=1),
            jnp.concatenate([jnp.zeros((WIDTH, WIDTH), F32), ds[2]], axis=1),
        ],
        axis=0,
    )
    ds_full = jnp.where(mask_s[...] > 0.5, ds_full, 0.0)
    db = triple(nn, ds_full, c_proj)
    dct = triple(nn, b_proj.T, ds_full)
    fgt[:WIDTH] = db.T.astype(BF16)
    fgt[WIDTH:state2] = dct.astype(BF16)
    fgt[state2:] = dlogit.astype(BF16)

    places = [(z, dx) for z in (other_z, z_at) for dx in (2, ahead, behind, 0)]
    twin_places = [(z, dx) for z in (other_z, z_at) for dx in (2, behind, ahead, 0)]
    n_core = {}

    def twin_part(slot):
        z, dx = twin_places[slot]
        index = index_of(z, x_at + dx, other_c)
        dwo[slot] = nn(fgt[...], hid[:, columns(index)]).astype(BF16)
        n_core[slot] = send(dwo.at[slot], from_core.at[slot], twin)

    def own_part(slot):
        z, dx = places[slot]
        index = index_of(z, x_at + dx, core)
        total = nn(fgt[...], hid[:, columns(index)])
        landed(from_core.at[slot], n_core[slot])
        return total + from_core[slot].astype(F32)

    def layer_part(index):
        spot = columns(index)
        w = wts[index]
        lay[:, spot] = (
            nt(fg[...], w[:state2]) + nn(fgl[:, :heads], w[state2:])
        ).astype(BF16)

    def ring_first(base, k):
        twin_part(base)
        twin_part(base + 1)
        acc[base] = own_part(base).astype(BF16)
        straight = send(acc.at[base, top], direct.at[k, top], opposite)
        hop = send(acc.at[base, low], hop1.at[k], fwd)
        twin_part(base + 2)
        plus = own_part(base + 1)
        acc[base + 1, top] = plus[:half].astype(BF16)
        keep[k] = plus[half:]
        f_t = send(acc.at[base + 1, top], hop2.at[k, 0, top], fwd)
        twin_part(base + 3)
        acc[base + 2] = own_part(base + 2).astype(BF16)
        b_t = send(acc.at[base + 2, top], hop2.at[k, 1, top], back)
        b_l = send(acc.at[base + 2, low], hop2.at[k, 1, low], back)
        zero_sum[k] = own_part(base + 3)
        return straight, hop, f_t, b_t, b_l

    def ring_next(base, k, hop):
        landed(hop1.at[k], hop)
        acc[base + 1, low] = (keep[k] + hop1[k].astype(F32)).astype(BF16)
        return send(acc.at[base + 1, low], hop2.at[k, 0, low], fwd)

    def ring_end(k, part, from_back, from_fwd):
        landed(hop2.at[k, 0, part], from_back)
        landed(hop2.at[k, 1, part], from_fwd)
        return (
            zero_sum[k, part, :]
            + hop2[k, 0, part, :].astype(F32)
            + hop2[k, 1, part, :].astype(F32)
        )

    def ring_top(k, straight, from_back, from_fwd):
        landed(direct.at[k, top], straight)
        return ring_end(k, top, from_back, from_fwd) + direct[k, top, :].astype(F32)

    twin_part(0)
    twin_part(1)
    acc[0] = own_part(0).astype(BF16)
    ways = ((0, direct.at[0], opposite), (1, hop2.at[0, 0], fwd), (2, hop2.at[0, 1], back))
    far = {}

    def straight_send(k, p):
        slot, into, device = ways[k]
        far[k, p] = send(acc.at[slot, halves[p]], into.at[halves[p]], device)

    straight_send(0, 0)
    twin_part(2)
    acc[1] = own_part(1).astype(BF16)
    straight_send(1, 0)
    twin_part(3)
    acc[2] = own_part(2).astype(BF16)
    straight_send(2, 0)
    for k in range(3):
        straight_send(k, 1)
    zero_sum[0] = own_part(3)
    straight2, hop, f_t2, b_t2, b_l2 = ring_first(4, 1)
    sums8 = exact(lambda a, b: nt(b, a), split3(stack), jnp.ones((8, chunk), BF16))
    heads_in[me] = sums8
    n_heads = [send(heads_in.at[me], heads_in.at[me], device) for device in peers]
    fg[:, :WIDTH] = db.astype(BF16)
    fg[:, WIDTH:] = dct.T.astype(BF16)
    wide = jnp.concatenate([dlogit, jnp.zeros((WIDTH - heads, chunk), F32)], axis=0)
    fgl[...] = wide.T.astype(BF16)
    for index in range(EARLY):
        layer_part(index)
    n_z = []
    for p, part in enumerate(halves):
        for k in range(3):
            landed(ways[k][1].at[part], far[k, p])
        zsend[part, :] = (
            zero_sum[0, part, :]
            + direct[0, part, :].astype(F32)
            + hop2[0, 0, part, :].astype(F32)
            + hop2[0, 1, part, :].astype(F32)
        ).astype(BF16)
        n_z.append(send(zsend.at[part], from_z.at[part], across))
    f_l2 = ring_next(4, 1, hop)

    for index in range(EARLY, seqs):
        layer_part(index)

    for k, number in enumerate(n_heads):
        landed(heads_in.at[lax.rem(me + seqs - k - 1, seqs)], number)
    head_grad = jnp.sum(heads_in[...], axis=0)[:1]
    head_own = head_own_s[:1]
    head_sq = jnp.sum(head_own * head_own, axis=1, keepdims=True) / (2 * heads)
    hgrad_sq = jnp.sum(head_grad * head_grad, axis=1, keepdims=True) / (2 * heads)
    head_trust = jnp.sqrt(head_sq) / jnp.sqrt(hgrad_sq + EPS)
    final_send[...] = jnp.broadcast_to(head_own - RATE * head_trust * head_grad, (8, WIDTH))
    n_final = send(final_send, part_s, mate)
    landed(part_p, n_part_p)

    def lanes_sum(value):
        total = jnp.sum(value * value, axis=0, keepdims=True)
        return total[:, :WIDTH] + total[:, WIDTH:]

    state_own = state_ref[...]
    step_own = step_ref[...]
    own_sq = [lanes_sum(state_own), lanes_sum(step_own)]
    mate_p = part_p[...].astype(F32)
    nstate_ref[...] = 0.5 * (state_own + mate_p[:state2])
    nstep_ref[...] = 0.5 * (step_own + mate_p[state2:])

    n_part_g = {}
    for q in range(2):
        spot = halves[q]
        if q:
            total = ring_end(1, low, f_l2, b_l2)
        else:
            total = ring_top(1, straight2, f_t2, b_t2)
        landed(from_z.at[spot], n_z[q])
        total = total + from_z[spot, :].astype(F32)
        grad_s[spot, :] = total
        gsend[spot, :] = total.astype(BF16)
        n_part_g[q] = send(gsend.at[spot], part_g.at[spot], mate)
    grad = grad_s[...]

    sums_in[me] = jnp.concatenate(
        [lanes_sum(grad[:state2]), lanes_sum(grad[state2:])]
        + own_sq
        + [jnp.zeros((4, WIDTH), F32)],
        axis=0,
    )
    n_sums = [send(sums_in.at[me], sums_in.at[me], device) for device in peers]
    n_mate = [
        send(sums_in.at[me], mate_sums.at[me], dict(mate, fsdp=lax.rem(me + k, seqs)))
        for k in range(seqs)
    ]
    grad_state = grad[:state2].T
    for q in range(2):
        landed(part_g.at[halves[q]], n_part_g[q])
    mate_g = part_g[...].astype(F32)
    mate_state = mate_g[:state2].T
    landed(part_s, n_final)
    head_mix = 0.5 * (final_send[:1] + part_s[:1])
    ndecay_ref[...] = head_mix[:, :heads]
    nbias_ref[...] = head_mix[:, heads : 2 * heads]
    for k, number in enumerate(n_sums):
        landed(sums_in.at[lax.rem(me + seqs - k - 1, seqs)], number)
    for k, number in enumerate(n_mate):
        landed(mate_sums.at[lax.rem(me + seqs - k, seqs)], number)
    width = seqs * chunk

    def trusts(ref):
        squares = jnp.sum(jnp.sum(ref[...], axis=0), axis=1, keepdims=True)
        state_trust = jnp.sqrt(squares[2:3] / (width * state2)) / jnp.sqrt(
            squares[0:1] / (width * state2) + EPS
        )
        step_trust = jnp.sqrt(squares[3:4] / (width * heads)) / jnp.sqrt(
            squares[1:2] / (width * heads) + EPS
        )
        return (0.5 * RATE) * state_trust, (0.5 * RATE) * step_trust

    state_trust, step_trust = trusts(sums_in)
    state_mate, step_mate = trusts(mate_sums)
    nstate_ref[...] -= state_trust * grad_state + state_mate * mate_state
    nstep_ref[...] -= step_trust * grad[state2:] + step_mate * mate_g[state2:]

    for copy in started:
        copy.wait_send()


def place_kernel(*refs):
    count = (len(refs) - 1) // 2
    sem = refs[-1]
    copies = [
        pltpu.make_async_copy(refs[k], refs[count + k], sem.at[k]) for k in range(count)
    ]
    for copy in copies:
        copy.start()
    for copy in copies:
        copy.wait()


def on_device(
    hidden_in, scan_in, grad_out, episodes, gossip_step, state_proj, step_proj, decay_log, step_bias
):
    reps = lax.axis_size("rep")
    seqs = lax.axis_size("fsdp")
    bits = reps.bit_length() - 1
    heads = step_proj.shape[1]
    length, inner = scan_in.shape[2:]
    model = hidden_in.shape[3]
    chunk = model // seqs
    state2 = 2 * WIDTH
    rows = state2 + heads
    half = rows // 2
    vmem = pl.BlockSpec(memory_space=pltpu.VMEM)
    anyspace = pl.BlockSpec(memory_space=pl.ANY)
    copies = 97
    shapes = (
        jax.ShapeDtypeStruct((length, model), BF16),
        jax.ShapeDtypeStruct((length, inner), BF16),
        jax.ShapeDtypeStruct((chunk, state2), F32),
        jax.ShapeDtypeStruct((heads, chunk), F32),
        jax.ShapeDtypeStruct((1, heads), F32),
        jax.ShapeDtypeStruct((1, heads), F32),
    )

    def run(bit, *operands):
        outs = pl.pallas_call(
            functools.partial(layer_kernel, (heads, seqs, chunk, rows, bit)),
            out_shape=shapes,
            in_specs=[anyspace] * 8,
            out_specs=(vmem,) * len(shapes),
            scratch_shapes=[
                pltpu.VMEM((chunk, state2), F32),
                pltpu.VMEM((heads, chunk), F32),
                pltpu.VMEM((1, length), jnp.int32),
                pltpu.VMEM((1, heads), F32),
                pltpu.VMEM((1, heads), F32),
                pltpu.VMEM((length, model), BF16),
                pltpu.VMEM((length, inner), BF16),
                pltpu.VMEM((length, inner), BF16),
                pltpu.VMEM((seqs, rows, chunk), BF16),
                pltpu.VMEM((heads, 3, WIDTH, WIDTH), F32),
                pltpu.VMEM((8, rows, chunk), BF16),
                pltpu.VMEM((8, rows, chunk), BF16),
                pltpu.VMEM((8, rows, chunk), BF16),
                pltpu.VMEM((2, half, chunk), BF16),
                pltpu.VMEM((2, rows, chunk), BF16),
                pltpu.VMEM((2, 2, rows, chunk), BF16),
                pltpu.VMEM((rows, chunk), BF16),
                pltpu.VMEM((rows, chunk), BF16),
                pltpu.VMEM((rows, chunk), BF16),
                pltpu.VMEM((8, WIDTH), F32),
                pltpu.VMEM((seqs, 8, WIDTH), F32),
                pltpu.VMEM((rows, chunk), BF16),
                pltpu.VMEM((rows, chunk), BF16),
                pltpu.VMEM((rows, chunk), F32),
                pltpu.VMEM((2, rows, chunk), F32),
                pltpu.VMEM((2, half, chunk), F32),
                pltpu.VMEM((seqs, 8, WIDTH), F32),
                pltpu.VMEM((seqs, 8, WIDTH), F32),
                pltpu.VMEM((8, WIDTH), F32),
                pltpu.VMEM((8, WIDTH), F32),
                pltpu.VMEM((length, state2), F32),
                pltpu.VMEM((length, WIDTH), F32),
                pltpu.VMEM((length, length), F32),
                pltpu.VMEM((length, WIDTH), F32),
                pltpu.VMEM((heads, 8, length), F32),
                pltpu.VMEM((3, WIDTH, WIDTH), F32),
                pltpu.VMEM((3, WIDTH, WIDTH), F32),
                pltpu.VMEM((2, 3, WIDTH, WIDTH), BF16),
                pltpu.VMEM((2, 3, WIDTH, WIDTH), BF16),
                pltpu.VMEM((heads, 8, length), F32),
                pltpu.VMEM((heads, 8, length), F32),
                pltpu.VMEM((rows, length), BF16),
                pltpu.VMEM((length, state2), BF16),
                pltpu.VMEM((length, WIDTH), BF16),
                pltpu.SemaphoreType.DMA((8,)),
                pltpu.SemaphoreType.DMA((copies,)),
                pltpu.SemaphoreType.DMA((copies,)),
            ],
            compiler_params=pltpu.CompilerParams(
                collective_id=bit, has_side_effects=True, vmem_limit_bytes=38 * 1024 * 1024
            ),
        )(*operands)
        return tuple(
            pl.pallas_call(
                place_kernel,
                out_shape=shapes,
                in_specs=[anyspace] * len(shapes),
                out_specs=(anyspace,) * len(shapes),
                scratch_shapes=[pltpu.SemaphoreType.DMA((len(shapes),))],
                compiler_params=pltpu.CompilerParams(vmem_limit_bytes=1024 * 1024),
            )(*outs)
        )

    operands = (
        state_proj[0],
        step_proj[0],
        episodes[0],
        decay_log,
        step_bias,
        hidden_in[0, 0],
        scan_in[0, 0],
        grad_out[0, 0],
    )
    outs = lax.switch(
        lax.rem(gossip_step[0], bits), [functools.partial(run, bit) for bit in range(bits)], *operands
    )
    layer_grad, scan_grad, new_state, new_step, new_decay, new_bias = outs
    return (
        layer_grad[None, None],
        scan_grad[None, None],
        new_state[None],
        new_step[None],
        new_decay,
        new_bias,
    )


def solution(mesh):
    in_specs = (
        P("rep", "fsdp", None, None),
        P("rep", "fsdp", None, None),
        P("rep", "fsdp", None, None),
        P("rep", "fsdp", None),
        P(),
        P("rep", "fsdp", None),
        P("rep", None, "fsdp"),
        P("rep", None),
        P("rep", None),
    )
    out_specs = (
        P("rep", "fsdp", None, None),
        P("rep", "fsdp", None, None),
        P("rep", "fsdp", None),
        P("rep", None, "fsdp"),
        P("rep", None),
        P("rep", None),
    )
    return jax.shard_map(
        on_device, mesh=mesh, in_specs=in_specs, out_specs=out_specs, check_vma=False
    )
```

```python
import functools

import jax
import jax.numpy as jnp
from jax import lax
from jax.experimental import pallas as pl
from jax.experimental.pallas import tpu as pltpu
from jax.sharding import PartitionSpec as P

MESH = pl.DeviceIdType.MESH
F32 = jnp.float32
BF16 = jnp.bfloat16
HIGH = lax.Precision.HIGHEST
LOG2E = 1.4426950408889634
TINY = 1e-37
CAP = 60.0
RATE = 0.1
EPS = 1e-6
WIDTH = 128
BARRIER_NEAR = True
EARLY = 10


def nn(a, b, precision=None):
    return lax.dot_general(
        a, b, (((1,), (0,)), ((), ())), precision=precision, preferred_element_type=F32
    )


def nt(a, b, precision=None):
    return lax.dot_general(
        a, b, (((1,), (1,)), ((), ())), precision=precision, preferred_element_type=F32
    )


def split3(value):
    high = value.astype(BF16).astype(F32)
    rest = value - high
    mid = rest.astype(BF16).astype(F32)
    return high, mid, rest - mid


def split2(value):
    high = value.astype(BF16)
    return high, (value - high.astype(F32)).astype(BF16)


def triple(product, a, b):
    ah, al = split2(a)
    bh, bl = split2(b)
    return product(ah, bh) + (product(ah, bl) + product(al, bh))


def exact(product, parts, b):
    high, mid, low = (part.astype(BF16) for part in parts)
    return product(high, b) + (product(mid, b) + product(low, b))


def layer_kernel(
    dims,
    state_hbm,
    step_hbm,
    ep_hbm,
    decay_hbm,
    bias_hbm,
    hid_hbm,
    val_hbm,
    cot_hbm,
    lay,
    sgr,
    nstate_ref,
    nstep_ref,
    ndecay_ref,
    nbias_ref,
    state_ref,
    step_ref,
    ep_ref,
    decay_ref,
    bias_ref,
    hid,
    val,
    cot,
    wts,
    gmat,
    dwo,
    acc,
    from_core,
    hop1,
    direct,
    hop2,
    from_z,
    part_p,
    part_g,
    part_s,
    mate_sums,
    zsend,
    gsend,
    grad_s,
    zero_sum,
    keep,
    heads_in,
    sums_in,
    final_send,
    head_own_s,
    feat,
    logit_s,
    mask_s,
    du_s,
    c2_s,
    scores,
    ds,
    vbuf,
    mbuf,
    mrow,
    mcol,
    fgt,
    fg,
    fgl,
    local_sem,
    ssem,
    rsem,
):
    heads, seqs, chunk, rows, bit = dims
    half = rows // 2
    state2 = 2 * WIDTH
    me = lax.axis_index("fsdp")
    rep = lax.axis_index("rep")
    core = lax.rem(me, 2)
    x_at = lax.rem(lax.div(me, 2), 4)
    z_at = lax.div(me, 8)

    def index_of(z, x, c):
        return z * 8 + lax.rem(x, 4) * 2 + c

    other_z = 1 - z_at
    other_c = 1 - core
    right = {"fsdp": index_of(z_at, x_at + 1, core)}
    left = {"fsdp": index_of(z_at, x_at + 3, core)}
    across = {"fsdp": index_of(other_z, x_at, core)}
    twin = {"fsdp": index_of(z_at, x_at, other_c)}
    ahead = 1 + 2 * core
    behind = 3 - 2 * core
    fwd = {"fsdp": index_of(z_at, x_at + ahead, core)}
    back = {"fsdp": index_of(z_at, x_at + behind, core)}
    opposite = {"fsdp": index_of(z_at, x_at + 2, core)}
    peers = [{"fsdp": lax.rem(me + k, seqs)} for k in range(1, seqs)]
    gap = 1 << bit
    mate = {"rep": rep + gap * (1 - 2 * lax.rem(lax.div(rep, gap), 2))}

    used = [0]
    started = []

    def remote(src, dst, number, device):
        return pltpu.make_async_remote_copy(
            src_ref=src,
            dst_ref=dst,
            send_sem=ssem.at[number],
            recv_sem=rsem.at[number],
            device_id=device,
            device_id_type=MESH,
        )

    def send(src, dst, device):
        number = used[0]
        used[0] += 1
        copy = remote(src, dst, number, device)
        copy.start()
        started.append(copy)
        return number

    def landed(dst, number):
        remote(dst, dst, number, twin).wait_recv()

    barrier = pltpu.get_barrier_semaphore()
    near = (twin, right, left, across, mate) if BARRIER_NEAR else peers + [mate]
    for device in near:
        pl.semaphore_signal(barrier, inc=1, device_id=device, device_id_type=MESH)
    small_loads = [
        pltpu.make_async_copy(src, dst, local_sem.at[3 + k])
        for k, (src, dst) in enumerate(
            (
                (state_hbm, state_ref),
                (step_hbm, step_ref),
                (ep_hbm, ep_ref),
                (decay_hbm, decay_ref),
                (bias_hbm, bias_ref),
            )
        )
    ]
    for load in small_loads:
        load.start()
    loads = [
        pltpu.make_async_copy(val_hbm, val, local_sem.at[0]),
        pltpu.make_async_copy(cot_hbm, cot, local_sem.at[1]),
        pltpu.make_async_copy(hid_hbm, hid, local_sem.at[2]),
    ]
    for load in loads:
        load.start()

    for load in small_loads:
        load.wait()
    wts[me, :state2] = state_ref[...].astype(BF16)
    wts[me, state2:] = step_ref[...].astype(BF16)
    at_u = lax.broadcasted_iota(jnp.int32, (chunk, chunk), 0)
    at_t = lax.broadcasted_iota(jnp.int32, (chunk, chunk), 1)
    ep_t = jnp.broadcast_to(ep_ref[...].astype(F32), (chunk, chunk))
    mask_s[...] = jnp.where((at_u <= at_t) & (ep_t.T == ep_t), 1.0, 0.0)
    eye_r = lax.broadcasted_iota(jnp.int32, (heads, heads), 0)
    eye_c = lax.broadcasted_iota(jnp.int32, (heads, heads), 1)

    def column(row_ref):
        spread_row = jnp.broadcast_to(row_ref[...], (heads, heads))
        return jnp.sum(jnp.where(eye_r == eye_c, spread_row, 0.0), axis=1, keepdims=True)

    decay = -jnp.exp(column(decay_ref))
    bias_col = column(bias_ref)
    place_r = lax.broadcasted_iota(jnp.int32, (heads, WIDTH), 0)
    place_c = lax.broadcasted_iota(jnp.int32, (heads, WIDTH), 1)
    place_d = jnp.where(place_c == place_r, 1.0, 0.0)
    place_b = jnp.where(place_c == place_r + heads, 1.0, 0.0)
    head_own_s[...] = nn(jnp.broadcast_to(decay_ref[...], (8, heads)), place_d, HIGH) + nn(
        jnp.broadcast_to(bias_ref[...], (8, heads)), place_b, HIGH
    )
    feat[...] = jnp.zeros_like(feat)
    logit_s[...] = jnp.zeros_like(logit_s)
    ds[...] = jnp.zeros_like(ds)

    def prepare(pair, carry):
        for k in range(2):
            h = pair * 2 + k
            lanes = pl.ds(pl.multiple_of(h * WIDTH, WIDTH), WIDTH)
            xh = val[:, lanes]
            gh = cot[:, lanes]
            first = nt(xh[:WIDTH], gh)
            gmat[h, 0] = first[:, :WIDTH]
            gmat[h, 1] = first[:, WIDTH:]
            gmat[h, 2] = nt(xh[WIDTH:], gh[WIDTH:])
        return carry

    pl.semaphore_wait(barrier, len(near))

    top = pl.ds(0, half)
    low = pl.ds(half, half)

    def pass_on(index, part, device):
        return send(wts.at[index, part], wts.at[index, part], device)

    def share(index):
        return send(wts.at[index], wts.at[index], twin)

    def columns(index):
        return pl.ds(pl.multiple_of(index * chunk, chunk), chunk)

    def feat_part(index):
        tokens = hid[:, columns(index)]
        feat[...] += nn(tokens, wts[index, :state2, :])
        logit_s[:, :heads] += nt(tokens, wts[index, state2:, :])

    def shared(z, dx, number):
        index = index_of(z, x_at + dx, other_c)
        landed(wts.at[index], number)
        feat_part(index)

    halves = (top, low)
    n_across = [pass_on(me, part, across) for part in halves]
    n_rt = pass_on(me, top, right)
    n_ll = pass_on(me, low, left)
    n_rl = pass_on(me, low, right)
    n_lt = pass_on(me, top, left)
    n_own = share(me)
    loads[0].wait()
    loads[1].wait()
    lax.fori_loop(0, heads // 2, prepare, 0)
    loads[2].wait()
    feat_part(me)
    shared(z_at, 0, n_own)

    def spread(z, n_rt, n_rl, n_ll, n_lt):
        at_l = index_of(z, x_at + 3, core)
        at_r = index_of(z, x_at + 1, core)
        landed(wts.at[at_l, top], n_rt)
        f_r = pass_on(at_l, top, right)
        landed(wts.at[at_r, low], n_ll)
        f_l = pass_on(at_r, low, left)
        landed(wts.at[at_l, low], n_rl)
        t_l = share(at_l)
        landed(wts.at[at_r, top], n_lt)
        t_r = share(at_r)
        return at_l, at_r, f_r, f_l, t_l, t_r

    at_l, at_r, f_r, f_l, t_l, t_r = spread(z_at, n_rt, n_rl, n_ll, n_lt)
    at_z = index_of(other_z, x_at, core)
    landed(wts.at[at_z, top], n_across[0])
    def scatter(part):
        return [pass_on(at_z, part, device) for device in (opposite, fwd, back)]

    far = [scatter(top)]
    landed(wts.at[at_z, low], n_across[1])
    far.append(scatter(low))
    t_z = share(at_z)
    feat_part(at_l)
    feat_part(at_r)
    at_2 = index_of(z_at, x_at + 2, core)
    landed(wts.at[at_2, top], f_r)
    landed(wts.at[at_2, low], f_l)
    t_2 = share(at_2)
    feat_part(at_z)
    feat_part(at_2)
    shared(z_at, 3, t_l)
    shared(z_at, 1, t_r)
    far_b = index_of(other_z, x_at + behind, core)
    far_f = index_of(other_z, x_at + ahead, core)
    far_2 = index_of(other_z, x_at + 2, core)
    far_own = (far_2, far_b, far_f)
    far_twin = (
        index_of(other_z, x_at + 2, other_c),
        index_of(other_z, x_at + ahead, other_c),
        index_of(other_z, x_at + behind, other_c),
    )
    shared(other_z, 0, t_z)
    shared(z_at, 2, t_2)
    t_far = {}
    for p, part in enumerate(halves):
        for k in (1, 2, 0):
            landed(wts.at[far_own[k], part], far[p][k])
            t_far[p, k] = pass_on(far_own[k], part, twin)
    for k in (1, 2, 0):
        feat_part(far_own[k])
    for k in (1, 2, 0):
        for p, part in enumerate(halves):
            landed(wts.at[far_twin[k], part], t_far[p, k])
        feat_part(far_twin[k])

    n_part_p = send(wts.at[me], part_p, mate)

    logits = logit_s[...].T[:heads] + bias_col
    small = jnp.exp(-jnp.abs(logits))
    log_part = jnp.where(
        small < 0.01, small * (1.0 - small * (0.5 - small * (1.0 / 3.0))), jnp.log(1.0 + small)
    )
    step = jnp.maximum(logits, 0.0) + log_part
    gate = jnp.where(logits >= 0.0, 1.0, small) / (1.0 + small)
    step_safe = jnp.maximum(step, TINY)
    ratio = jnp.where(logits < -20.0, 1.0, gate / step_safe)
    upper = jnp.where(at_u <= at_t, 1.0, 0.0).astype(BF16)
    c2 = exact(nn, split3(decay * step), upper) * LOG2E
    du = jnp.log2(step_safe) - c2
    du_s[...] = jnp.concatenate([du, jnp.zeros((WIDTH - heads, chunk), F32)], axis=0).T
    c2_s[:, 0, :] = c2
    b_proj = feat[:, :WIDTH]
    c_proj = feat[:, WIDTH:]
    masked = jnp.where(mask_s[...] > 0.5, triple(nt, b_proj, c_proj), 0.0)
    scores[0] = masked[:WIDTH, :WIDTH]
    scores[1] = masked[:WIDTH, WIDTH:]
    scores[2] = masked[WIDTH:, WIDTH:]
    ones8 = jnp.ones((8, chunk), BF16)

    def weigh(h, lane, slot):
        row = c2_s[h, 0:1, :]
        first = jnp.broadcast_to(du_s[:WIDTH, lane : lane + 1], (WIDTH, WIDTH))
        second = jnp.broadcast_to(du_s[WIDTH:, lane : lane + 1], (WIDTH, WIDTH))
        args = (
            jnp.minimum(first + row[:, :WIDTH], CAP),
            first + row[:, WIDTH:],
            jnp.minimum(second + row[:, WIDTH:], CAP),
        )
        for k in range(3):
            e = jnp.exp2(args[k])
            p = gmat[h, k] * e
            ds[k] += p
            vbuf[slot, k] = (e * scores[k]).astype(BF16)
            mbuf[slot, k] = (p * scores[k]).astype(BF16)

    def apply(h, slot):
        lanes = pl.ds(pl.multiple_of(h * WIDTH, WIDTH), WIDTH)
        gh = cot[:, lanes]
        v0 = jnp.concatenate([vbuf[slot, 0], vbuf[slot, 1]], axis=1)
        sgr[:WIDTH, lanes] = nn(v0, gh).astype(BF16)
        sgr[WIDTH:, lanes] = nn(vbuf[slot, 2], gh[WIDTH:]).astype(BF16)
        m0 = jnp.concatenate([mbuf[slot, 0], mbuf[slot, 1]], axis=1)
        m1 = jnp.concatenate([mbuf[slot, 1], mbuf[slot, 2]], axis=0)
        mrow[h, :, :WIDTH] = nn(ones8[:, :WIDTH], mbuf[slot, 0])
        mrow[h, :, WIDTH:] = nn(ones8, m1)
        mcol[h, :, :WIDTH] = nt(ones8, m0)
        mcol[h, :, WIDTH:] = nt(ones8[:, :WIDTH], mbuf[slot, 2])

    weigh(0, 0, 0)

    def head_pair(pair, carry):
        h = pair * 2
        weigh(h + 1, 1, 1)
        apply(h, 0)
        weigh(h + 2, 2, 0)
        apply(h + 1, 1)
        du_s[...] = pltpu.roll(du_s[...], WIDTH - 2, 1)
        return carry

    lax.fori_loop(0, heads // 2 - 1, head_pair, 0)
    weigh(heads - 1, 1, 1)
    apply(heads - 2, 0)
    apply(heads - 1, 1)

    lower = jnp.where(at_u >= at_t, 1.0, 0.0).astype(BF16)
    mc = jnp.sum(mcol[...], axis=1) * 0.125
    drate = exact(nn, split3(jnp.sum(mrow[...], axis=1) * 0.125 - mc), lower)
    dlogit = mc * ratio + gate * (decay * drate)
    ddecay = decay * step * drate
    stack = jnp.concatenate(
        [ddecay, dlogit, jnp.zeros((WIDTH - 2 * heads, chunk), F32)], axis=0
    )
    ds_full = jnp.concatenate(
        [
            jnp.concatenate([ds[0], ds[1]], axis=1),
            jnp.concatenate([jnp.zeros((WIDTH, WIDTH), F32), ds[2]], axis=1),
        ],
        axis=0,
    )
    ds_full = jnp.where(mask_s[...] > 0.5, ds_full, 0.0)
    db = triple(nn, ds_full, c_proj)
    dct = triple(nn, b_proj.T, ds_full)
    fgt[:WIDTH] = db.T.astype(BF16)
    fgt[WIDTH:state2] = dct.astype(BF16)
    fgt[state2:] = dlogit.astype(BF16)

    places = [(z, dx) for z in (other_z, z_at) for dx in (2, ahead, behind, 0)]
    twin_places = [(z, dx) for z in (other_z, z_at) for dx in (2, behind, ahead, 0)]
    n_core = {}

    def twin_part(slot):
        z, dx = twin_places[slot]
        index = index_of(z, x_at + dx, other_c)
        dwo[slot] = nn(fgt[...], hid[:, columns(index)]).astype(BF16)
        n_core[slot] = send(dwo.at[slot], from_core.at[slot], twin)

    def own_part(slot):
        z, dx = places[slot]
        index = index_of(z, x_at + dx, core)
        total = nn(fgt[...], hid[:, columns(index)])
        landed(from_core.at[slot], n_core[slot])
        return total + from_core[slot].astype(F32)

    def layer_part(index):
        spot = columns(index)
        w = wts[index]
        lay[:, spot] = (
            nt(fg[...], w[:state2]) + nn(fgl[:, :heads], w[state2:])
        ).astype(BF16)

    def ring_first(base, k):
        twin_part(base)
        twin_part(base + 1)
        acc[base] = own_part(base).astype(BF16)
        straight = send(acc.at[base, top], direct.at[k, top], opposite)
        hop = send(acc.at[base, low], hop1.at[k], fwd)
        twin_part(base + 2)
        plus = own_part(base + 1)
        acc[base + 1, top] = plus[:half].astype(BF16)
        keep[k] = plus[half:]
        f_t = send(acc.at[base + 1, top], hop2.at[k, 0, top], fwd)
        twin_part(base + 3)
        acc[base + 2] = own_part(base + 2).astype(BF16)
        b_t = send(acc.at[base + 2, top], hop2.at[k, 1, top], back)
        b_l = send(acc.at[base + 2, low], hop2.at[k, 1, low], back)
        zero_sum[k] = own_part(base + 3)
        return straight, hop, f_t, b_t, b_l

    def ring_next(base, k, hop):
        landed(hop1.at[k], hop)
        acc[base + 1, low] = (keep[k] + hop1[k].astype(F32)).astype(BF16)
        return send(acc.at[base + 1, low], hop2.at[k, 0, low], fwd)

    def ring_end(k, part, from_back, from_fwd):
        landed(hop2.at[k, 0, part], from_back)
        landed(hop2.at[k, 1, part], from_fwd)
        return (
            zero_sum[k, part, :]
            + hop2[k, 0, part, :].astype(F32)
            + hop2[k, 1, part, :].astype(F32)
        )

    def ring_top(k, straight, from_back, from_fwd):
        landed(direct.at[k, top], straight)
        return ring_end(k, top, from_back, from_fwd) + direct[k, top, :].astype(F32)

    twin_part(0)
    twin_part(1)
    acc[0] = own_part(0).astype(BF16)
    ways = ((0, direct.at[0], opposite), (1, hop2.at[0, 0], fwd), (2, hop2.at[0, 1], back))
    far = {}

    def straight_send(k, p):
        slot, into, device = ways[k]
        far[k, p] = send(acc.at[slot, halves[p]], into.at[halves[p]], device)

    straight_send(0, 0)
    twin_part(2)
    acc[1] = own_part(1).astype(BF16)
    straight_send(1, 0)
    twin_part(3)
    acc[2] = own_part(2).astype(BF16)
    straight_send(2, 0)
    for k in range(3):
        straight_send(k, 1)
    zero_sum[0] = own_part(3)
    sums8 = exact(lambda a, b: nt(b, a), split3(stack), jnp.ones((8, chunk), BF16))
    heads_in[me] = sums8
    n_heads = [send(heads_in.at[me], heads_in.at[me], device) for device in peers]
    fg[:, :WIDTH] = db.astype(BF16)
    fg[:, WIDTH:] = dct.T.astype(BF16)
    wide = jnp.concatenate([dlogit, jnp.zeros((WIDTH - heads, chunk), F32)], axis=0)
    fgl[...] = wide.T.astype(BF16)
    for index in range(EARLY):
        layer_part(index)
    straight2, hop, f_t2, b_t2, b_l2 = ring_first(4, 1)
    n_z = []
    for p, part in enumerate(halves):
        for k in range(3):
            landed(ways[k][1].at[part], far[k, p])
        zsend[part, :] = (
            zero_sum[0, part, :]
            + direct[0, part, :].astype(F32)
            + hop2[0, 0, part, :].astype(F32)
            + hop2[0, 1, part, :].astype(F32)
        ).astype(BF16)
        n_z.append(send(zsend.at[part], from_z.at[part], across))
    f_l2 = ring_next(4, 1, hop)

    for index in range(EARLY, seqs):
        layer_part(index)

    for k, number in enumerate(n_heads):
        landed(heads_in.at[lax.rem(me + seqs - k - 1, seqs)], number)
    head_grad = jnp.sum(heads_in[...], axis=0)[:1]
    head_own = head_own_s[:1]
    head_sq = jnp.sum(head_own * head_own, axis=1, keepdims=True) / (2 * heads)
    hgrad_sq = jnp.sum(head_grad * head_grad, axis=1, keepdims=True) / (2 * heads)
    head_trust = jnp.sqrt(head_sq) / jnp.sqrt(hgrad_sq + EPS)
    final_send[...] = jnp.broadcast_to(head_own - RATE * head_trust * head_grad, (8, WIDTH))
    n_final = send(final_send, part_s, mate)
    landed(part_p, n_part_p)

    def lanes_sum(value):
        total = jnp.sum(value * value, axis=0, keepdims=True)
        return total[:, :WIDTH] + total[:, WIDTH:]

    state_own = state_ref[...]
    step_own = step_ref[...]
    own_sq = [lanes_sum(state_own), lanes_sum(step_own)]
    mate_p = part_p[...].astype(F32)
    nstate_ref[...] = 0.5 * (state_own + mate_p[:state2])
    nstep_ref[...] = 0.5 * (step_own + mate_p[state2:])

    n_part_g = {}
    for q in range(2):
        spot = halves[q]
        if q:
            total = ring_end(1, low, f_l2, b_l2)
        else:
            total = ring_top(1, straight2, f_t2, b_t2)
        landed(from_z.at[spot], n_z[q])
        total = total + from_z[spot, :].astype(F32)
        grad_s[spot, :] = total
        gsend[spot, :] = total.astype(BF16)
        n_part_g[q] = send(gsend.at[spot], part_g.at[spot], mate)
    grad = grad_s[...]

    sums_in[me] = jnp.concatenate(
        [lanes_sum(grad[:state2]), lanes_sum(grad[state2:])]
        + own_sq
        + [jnp.zeros((4, WIDTH), F32)],
        axis=0,
    )
    n_sums = [send(sums_in.at[me], sums_in.at[me], device) for device in peers]
    n_mate = [
        send(sums_in.at[me], mate_sums.at[me], dict(mate, fsdp=lax.rem(me + k, seqs)))
        for k in range(seqs)
    ]
    grad_state = grad[:state2].T
    for q in range(2):
        landed(part_g.at[halves[q]], n_part_g[q])
    mate_g = part_g[...].astype(F32)
    mate_state = mate_g[:state2].T
    landed(part_s, n_final)
    head_mix = 0.5 * (final_send[:1] + part_s[:1])
    ndecay_ref[...] = head_mix[:, :heads]
    nbias_ref[...] = head_mix[:, heads : 2 * heads]
    for k, number in enumerate(n_sums):
        landed(sums_in.at[lax.rem(me + seqs - k - 1, seqs)], number)
    for k, number in enumerate(n_mate):
        landed(mate_sums.at[lax.rem(me + seqs - k, seqs)], number)
    width = seqs * chunk

    def trusts(ref):
        squares = jnp.sum(jnp.sum(ref[...], axis=0), axis=1, keepdims=True)
        state_trust = jnp.sqrt(squares[2:3] / (width * state2)) / jnp.sqrt(
            squares[0:1] / (width * state2) + EPS
        )
        step_trust = jnp.sqrt(squares[3:4] / (width * heads)) / jnp.sqrt(
            squares[1:2] / (width * heads) + EPS
        )
        return (0.5 * RATE) * state_trust, (0.5 * RATE) * step_trust

    state_trust, step_trust = trusts(sums_in)
    state_mate, step_mate = trusts(mate_sums)
    nstate_ref[...] -= state_trust * grad_state + state_mate * mate_state
    nstep_ref[...] -= step_trust * grad[state2:] + step_mate * mate_g[state2:]

    for copy in started:
        copy.wait_send()


def place_kernel(*refs):
    count = (len(refs) - 1) // 2
    sem = refs[-1]
    copies = [
        pltpu.make_async_copy(refs[k], refs[count + k], sem.at[k]) for k in range(count)
    ]
    for copy in copies:
        copy.start()
    for copy in copies:
        copy.wait()


def on_device(
    hidden_in, scan_in, grad_out, episodes, gossip_step, state_proj, step_proj, decay_log, step_bias
):
    reps = lax.axis_size("rep")
    seqs = lax.axis_size("fsdp")
    bits = reps.bit_length() - 1
    heads = step_proj.shape[1]
    length, inner = scan_in.shape[2:]
    model = hidden_in.shape[3]
    chunk = model // seqs
    state2 = 2 * WIDTH
    rows = state2 + heads
    half = rows // 2
    vmem = pl.BlockSpec(memory_space=pltpu.VMEM)
    anyspace = pl.BlockSpec(memory_space=pl.ANY)
    copies = 97
    shapes = (
        jax.ShapeDtypeStruct((length, model), BF16),
        jax.ShapeDtypeStruct((length, inner), BF16),
        jax.ShapeDtypeStruct((chunk, state2), F32),
        jax.ShapeDtypeStruct((heads, chunk), F32),
        jax.ShapeDtypeStruct((1, heads), F32),
        jax.ShapeDtypeStruct((1, heads), F32),
    )

    def run(bit, *operands):
        outs = pl.pallas_call(
            functools.partial(layer_kernel, (heads, seqs, chunk, rows, bit)),
            out_shape=shapes,
            in_specs=[anyspace] * 8,
            out_specs=(vmem,) * len(shapes),
            scratch_shapes=[
                pltpu.VMEM((chunk, state2), F32),
                pltpu.VMEM((heads, chunk), F32),
                pltpu.VMEM((1, length), jnp.int32),
                pltpu.VMEM((1, heads), F32),
                pltpu.VMEM((1, heads), F32),
                pltpu.VMEM((length, model), BF16),
                pltpu.VMEM((length, inner), BF16),
                pltpu.VMEM((length, inner), BF16),
                pltpu.VMEM((seqs, rows, chunk), BF16),
                pltpu.VMEM((heads, 3, WIDTH, WIDTH), F32),
                pltpu.VMEM((8, rows, chunk), BF16),
                pltpu.VMEM((8, rows, chunk), BF16),
                pltpu.VMEM((8, rows, chunk), BF16),
                pltpu.VMEM((2, half, chunk), BF16),
                pltpu.VMEM((2, rows, chunk), BF16),
                pltpu.VMEM((2, 2, rows, chunk), BF16),
                pltpu.VMEM((rows, chunk), BF16),
                pltpu.VMEM((rows, chunk), BF16),
                pltpu.VMEM((rows, chunk), BF16),
                pltpu.VMEM((8, WIDTH), F32),
                pltpu.VMEM((seqs, 8, WIDTH), F32),
                pltpu.VMEM((rows, chunk), BF16),
                pltpu.VMEM((rows, chunk), BF16),
                pltpu.VMEM((rows, chunk), F32),
                pltpu.VMEM((2, rows, chunk), F32),
                pltpu.VMEM((2, half, chunk), F32),
                pltpu.VMEM((seqs, 8, WIDTH), F32),
                pltpu.VMEM((seqs, 8, WIDTH), F32),
                pltpu.VMEM((8, WIDTH), F32),
                pltpu.VMEM((8, WIDTH), F32),
                pltpu.VMEM((length, state2), F32),
                pltpu.VMEM((length, WIDTH), F32),
                pltpu.VMEM((length, length), F32),
                pltpu.VMEM((length, WIDTH), F32),
                pltpu.VMEM((heads, 8, length), F32),
                pltpu.VMEM((3, WIDTH, WIDTH), F32),
                pltpu.VMEM((3, WIDTH, WIDTH), F32),
                pltpu.VMEM((2, 3, WIDTH, WIDTH), BF16),
                pltpu.VMEM((2, 3, WIDTH, WIDTH), BF16),
                pltpu.VMEM((heads, 8, length), F32),
                pltpu.VMEM((heads, 8, length), F32),
                pltpu.VMEM((rows, length), BF16),
                pltpu.VMEM((length, state2), BF16),
                pltpu.VMEM((length, WIDTH), BF16),
                pltpu.SemaphoreType.DMA((8,)),
                pltpu.SemaphoreType.DMA((copies,)),
                pltpu.SemaphoreType.DMA((copies,)),
            ],
            compiler_params=pltpu.CompilerParams(
                collective_id=bit, has_side_effects=True, vmem_limit_bytes=38 * 1024 * 1024
            ),
        )(*operands)
        return tuple(
            pl.pallas_call(
                place_kernel,
                out_shape=shapes,
                in_specs=[anyspace] * len(shapes),
                out_specs=(anyspace,) * len(shapes),
                scratch_shapes=[pltpu.SemaphoreType.DMA((len(shapes),))],
                compiler_params=pltpu.CompilerParams(vmem_limit_bytes=1024 * 1024),
            )(*outs)
        )

    operands = (
        state_proj[0],
        step_proj[0],
        episodes[0],
        decay_log,
        step_bias,
        hidden_in[0, 0],
        scan_in[0, 0],
        grad_out[0, 0],
    )
    outs = lax.switch(
        lax.rem(gossip_step[0], bits), [functools.partial(run, bit) for bit in range(bits)], *operands
    )
    layer_grad, scan_grad, new_state, new_step, new_decay, new_bias = outs
    return (
        layer_grad[None, None],
        scan_grad[None, None],
        new_state[None],
        new_step[None],
        new_decay,
        new_bias,
    )


def solution(mesh):
    in_specs = (
        P("rep", "fsdp", None, None),
        P("rep", "fsdp", None, None),
        P("rep", "fsdp", None, None),
        P("rep", "fsdp", None),
        P(),
        P("rep", "fsdp", None),
        P("rep", None, "fsdp"),
        P("rep", None),
        P("rep", None),
    )
    out_specs = (
        P("rep", "fsdp", None, None),
        P("rep", "fsdp", None, None),
        P("rep", "fsdp", None),
        P("rep", None, "fsdp"),
        P("rep", None),
        P("rep", None),
    )
    return jax.shard_map(
        on_device, mesh=mesh, in_specs=in_specs, out_specs=out_specs, check_vma=False
    )
```
